32 devices in a mesh: row: 4 (over x, core), col: 8 (over z, y).
Axes of the slice: x: 2, y: 2, z: 4, core: 2. Of those that a mesh axis runs over, the one named last changes fastest.
Arguments:
- hidden_in: bfloat16 [4, 8, 512, 896], P('row', 'col'), may hold values from -6 to 6
- targets: bfloat16 [4, 8, 512, 896], P('row', 'col'), may hold values from -6 to 6
- first_params: float32 [4, 896, 896], P('row', 'col'), may hold values from -0.1875 to 0.1875
- first_moment: float32 [4, 896, 896], P('row', 'col'), may hold values from -0.06 to 0.06
- second_params: float32 [8, 896, 896], P('col', 'row'), may hold values from -0.1875 to 0.1875
- second_moment: float32 [8, 896, 896], P('col', 'row'), may hold values from -0.06 to 0.06
Outputs:
- first_params_new: float32 [4, 896, 896], P('row', 'col')
- first_moment_new: float32 [4, 896, 896], P('row', 'col')
- second_params_new: float32 [8, 896, 896], P('col', 'row')
- second_moment_new: float32 [8, 896, 896], P('col', 'row')
The draws below stay inside these ranges and needn't reach their ends.
All inputs are finite; a program needn't handle non-finite values.
Results may differ from the reference program's by a relative error of at most 0.022.
Values may be sent and summed in bfloat16 or wider, within the bound.
No kernel may reach another device: no remote copies, remote signals or barrier semaphores. Data moves between devices by JAX's collectives and lax.ppermute only.
A program may use at most 64 MiB of HBM per device.

```python
import jax
import jax.numpy as jnp
from jax import lax

D = 896
TOK_DEV = 512
SHIFT = 2
N_ROW = 4
N_COL = 8


def block_levels(rng, dims, shards, least, high):
    loudness = 1.0
    for dim, shards_of in shards:
        steps = jax.random.uniform(jax.random.fold_in(jax.random.fold_in(rng, 6), dim), (shards_of,), jnp.float32, least / len(shards), high / len(shards))
        loudness = loudness * jnp.repeat(jnp.exp(steps), dims[dim] // shards_of).reshape((-1,) + (1,) * (len(dims) - 1 - dim))
    return loudness


def noise(key, shape, spread, limit, shards=(), kind=jnp.bfloat16):
    result = jax.random.normal(key, shape, jnp.float32) * spread
    if len(shards) > 0:
        result = block_levels(key, shape, shards, -0.22, 0.18) * result
    return jnp.clip(result, min=-limit, max=limit).astype(kind)


def setup_inputs(seed: int = 0) -> dict:
    key_of = jax.random.split(jax.random.key(seed), 7)
    hidden_in = noise(key_of[0], (N_ROW, N_COL, TOK_DEV, D), 1.0, 6.0, ((0, 4), (1, 8)))
    targets = noise(key_of[1], (N_ROW, N_COL, TOK_DEV, D), 1.0, 6.0, ((0, 4), (1, 8)))
    first_params = noise(key_of[2], (N_ROW, D, D), D ** -0.5, 0.1875, ((0, 4), (1, 8)), jnp.float32)
    first_moment = noise(key_of[3], (N_ROW, D, D), 0.01, 0.06, ((0, 4), (1, 8)), jnp.float32)
    second_params = noise(key_of[4], (N_COL, D, D), D ** -0.5, 0.1875, ((0, 8), (1, 4)), jnp.float32)
    second_moment = noise(key_of[5], (N_COL, D, D), 0.01, 0.06, ((0, 8), (1, 4)), jnp.float32)
    return dict(hidden_in=hidden_in, targets=targets, first_params=first_params, first_moment=first_moment, second_params=second_params, second_moment=second_moment)


outer_momentum = 0.9
outer_rate = 0.7

def gelu_tanh(value):
    return jax.nn.gelu(value, approximate=True)

def path_grads(inputs, wanted, first_b, second_b):
    pre = jnp.dot(inputs, first_b, preferred_element_type=jnp.float32)
    active, slope = jax.vjp(gelu_tanh, pre)
    active_b = active.astype(jnp.bfloat16)
    output = jnp.dot(active_b, second_b, preferred_element_type=jnp.float32)
    error = ((output - wanted.astype(jnp.float32)) / TOK_DEV).astype(jnp.bfloat16)
    back = lax.dot_general(error, second_b, (((1,), (1,)), ((), ())), preferred_element_type=jnp.float32)
    grad_pre = slope(back)[0].astype(jnp.bfloat16)
    path_second = lax.dot_general(active_b, error, (((0,), (0,)), ((), ())), preferred_element_type=jnp.float32)
    path_first = lax.dot_general(inputs, grad_pre, (((0,), (0,)), ((), ())), preferred_element_type=jnp.float32)
    path_first = lax.optimization_barrier(path_first.astype(jnp.bfloat16)).astype(jnp.float32)
    path_second = lax.optimization_barrier(path_second.astype(jnp.bfloat16)).astype(jnp.float32)
    return (path_first, path_second)

def nesterov(params, moment, grad):
    moment_new = outer_momentum * moment + grad
    return (params - outer_rate * (grad + outer_momentum * moment_new), moment_new)

def reference(hidden_in, targets, first_params, first_moment, second_params, second_moment):
    first_b = first_params.astype(jnp.bfloat16)
    second_b = second_params.astype(jnp.bfloat16)

    def one_path(carry, index):
        first_total, second_total = carry
        row_index = index // N_COL
        col_index = index % N_COL
        path_first, path_second = path_grads(hidden_in[row_index, col_index], targets[row_index, col_index], first_b[row_index], second_b[col_index])
        first_total = first_total.at[row_index].add(path_first)
        second_total = second_total.at[col_index].add(path_second)
        return ((first_total, second_total), None)
    start = (jnp.zeros(first_params.shape, jnp.float32), jnp.zeros(second_params.shape, jnp.float32))
    (first_total, second_total), unused = lax.scan(one_path, start, jnp.arange(N_ROW * N_COL, dtype=jnp.int32))
    first_grad = first_total / N_COL
    second_grad = second_total / N_ROW
    first_params_new, first_moment_new = nesterov(first_params, first_moment, first_grad)
    second_upd, second_mom = nesterov(second_params, second_moment, second_grad)
    second_params_new = jnp.roll(second_upd, SHIFT, axis=0)
    second_moment_new = jnp.roll(second_mom, SHIFT, axis=0)
    return (first_params_new, first_moment_new, second_params_new, second_moment_new)
```

```python
import jax
import jax.numpy as jnp
from jax import lax
from jax.sharding import PartitionSpec as P

outer_momentum = 0.9
outer_rate = 0.7


def passed_along(x, axis, by):
    length = lax.axis_size(axis)
    return lax.ppermute(x, axis, [(i, (i + by) % length) for i in range(length)])


def gelu_tanh(value):
    return jax.nn.gelu(value, approximate=True)


def nesterov(params, moment, grad):
    moment_new = outer_momentum * moment + grad
    return (params - outer_rate * (grad + outer_momentum * moment_new), moment_new)


def snake(length):
    return list(range(0, length, 2)) + list(range(length - 1, 0, -2))


def place_of(member, length):
    return jnp.where(member % 2 == 0, member // 2, length - 1 - member // 2)


def member_at(place, length):
    place = lax.rem(place + 2 * length, length)
    return jnp.where(place < length // 2, 2 * place, 2 * (length - 1 - place) + 1)


def ring_pairs(length):
    order = snake(length)
    up = [(order[i], order[(i + 1) % length]) for i in range(length)]
    return up, [(b, a) for a, b in up]


def ring_gather(shard, axis):
    length = lax.axis_size(axis)
    rows = shard.shape[0]
    half = rows // 2
    up, down = ring_pairs(length)
    place = place_of(lax.axis_index(axis), length)
    full = jnp.zeros((rows * length,) + shard.shape[1:], shard.dtype)

    def put(full, block, back, offset=0):
        return lax.dynamic_update_slice(
            full, block, (member_at(place + back, length) * rows + offset, 0)
        )

    full = put(full, shard, 0)
    forward = backward = shard
    for step in range(1, length // 2 + 1):
        if step == length // 2:
            forward, backward = forward[:half], backward[half:]
        forward = lax.ppermute(forward, axis, up)
        backward = lax.ppermute(backward, axis, down)
        full = put(full, forward, -step)
        full = put(full, backward, step, half if step == length // 2 else 0)
    return full


def ring_scatter(parts, axis):
    length = lax.axis_size(axis)
    up, down = ring_pairs(length)
    term = parts(length // 2)
    half = term.shape[0] // 2
    forward = lax.ppermute(term[:half].astype(jnp.bfloat16), axis, up)
    backward = lax.ppermute(term[half:].astype(jnp.bfloat16), axis, down)
    for left in range(length // 2 - 1, 0, -1):
        ahead, behind = parts(left), parts(-left)
        if left == length // 2 - 1:
            zero = jnp.zeros_like(forward)
            forward = jnp.concatenate([forward, zero])
            backward = jnp.concatenate([zero, backward])
        forward = (ahead + forward.astype(jnp.float32)).astype(jnp.bfloat16)
        backward = (behind + backward.astype(jnp.float32)).astype(jnp.bfloat16)
        forward = lax.ppermute(forward, axis, up)
        backward = lax.ppermute(backward, axis, down)
    return parts(0) + forward.astype(jnp.float32) + backward.astype(jnp.float32)


def doubling_gather(shard, axis):
    length = lax.axis_size(axis)
    me = lax.axis_index(axis)
    rows = shard.shape[0]
    held = shard[None]
    members = [me]
    bit = length // 2
    while bit >= 1:
        other = lax.ppermute(held, axis, [(i, i ^ bit) for i in range(length)])
        held = jnp.concatenate([held, other])
        members = members + [m ^ bit for m in members]
        bit //= 2
    full = jnp.zeros((rows * length,) + shard.shape[1:], shard.dtype)
    for k, member in enumerate(members):
        full = lax.dynamic_update_slice(full, held[k], (member * rows, 0))
    return full


def halving_scatter(terms, axis):
    length = lax.axis_size(axis)
    me = lax.axis_index(axis)
    rows = terms.shape[0] // length
    held = terms.reshape((length, rows) + terms.shape[1:])
    bit = 1
    while bit < length:
        mine = (me // bit) % 2
        pairs = held.reshape((held.shape[0] // 2, 2) + held.shape[1:])
        away = lax.dynamic_index_in_dim(pairs, 1 - mine, 1, keepdims=False)
        kept = lax.dynamic_index_in_dim(pairs, mine, 1, keepdims=False)
        came = lax.ppermute(away.astype(jnp.bfloat16), axis, [(i, i ^ bit) for i in range(length)])
        held = kept.astype(jnp.float32) + came.astype(jnp.float32)
        bit *= 2
    return held[0]


def per_device(hidden_in, targets, first_params, first_moment, second_params, second_moment):
    inputs = hidden_in[0, 0]
    wanted = targets[0, 0]
    tokens = inputs.shape[0]
    columns = lax.axis_size("col")
    offset = columns // 4
    first_full = ring_gather(first_params[0].astype(jnp.bfloat16), "col")
    second_full = doubling_gather(second_params[0].astype(jnp.bfloat16), "row")
    pre = jnp.dot(inputs, first_full, preferred_element_type=jnp.float32)
    active, slope = jax.vjp(gelu_tanh, pre)
    active_b = active.astype(jnp.bfloat16)
    output = jnp.dot(active_b, second_full, preferred_element_type=jnp.float32)
    error = ((output - wanted.astype(jnp.float32)) / tokens).astype(jnp.bfloat16)
    path_second = lax.dot_general(
        active_b, error, (((0,), (0,)), ((), ())), preferred_element_type=jnp.float32
    ).astype(jnp.bfloat16)
    second_grad = halving_scatter(path_second, "row") / lax.axis_size("row")
    back = lax.dot_general(
        error, second_full, (((1,), (1,)), ((), ())), preferred_element_type=jnp.float32
    )
    grad_pre = slope(back)[0].astype(jnp.bfloat16)
    path_first = lax.dot_general(
        inputs, grad_pre, (((0,), (0,)), ((), ())), preferred_element_type=jnp.float32
    ).astype(jnp.bfloat16)
    rows = first_params.shape[1]
    place = place_of(lax.axis_index("col"), columns)

    def part(away):
        block = lax.dynamic_slice_in_dim(path_first, member_at(place + away, columns) * rows, rows, 0)
        return block.astype(jnp.float32)

    first_grad = ring_scatter(part, "col") / columns
    first_params_new, first_moment_new = nesterov(first_params, first_moment, first_grad[None])
    second_upd, second_mom = nesterov(second_params, second_moment, second_grad[None])
    stacked = jnp.stack([second_upd, second_mom])
    moved = passed_along(stacked.astype(jnp.bfloat16), "col", offset).astype(stacked.dtype)
    return (first_params_new, first_moment_new, moved[0], moved[1])


def solution(mesh):
    return jax.shard_map(
        per_device,
        mesh=mesh,
        in_specs=(
            P("row", "col", None, None),
            P("row", "col", None, None),
            P("row", "col", None),
            P("row", "col", None),
            P("col", "row", None),
            P("col", "row", None),
        ),
        out_specs=(
            P("row", "col", None),
            P("row", "col", None),
            P("col", "row", None),
            P("col", "row", None),
        ),
        check_vma=False,
    )
```

```python
import math

import jax
import jax.numpy as jnp
from jax import lax
from jax.experimental import pallas as pl
from jax.experimental.pallas import tpu as pltpu
from jax.sharding import PartitionSpec as P

outer_momentum = 0.9
outer_rate = 0.7
BF16 = jnp.bfloat16
F32 = jnp.float32
WHOLE = pl.BlockSpec(memory_space=pltpu.VMEM)


def shape_of(shape, kind=BF16):
    return jax.ShapeDtypeStruct(shape, kind)


def call(kernel, outs, scratch, *operands, flops=0):
    moved = sum(o.size * o.dtype.itemsize for o in operands)
    return pl.pallas_call(
        kernel,
        out_shape=tuple(outs),
        in_specs=[WHOLE] * len(operands),
        out_specs=(WHOLE,) * len(outs),
        scratch_shapes=scratch,
        compiler_params=pltpu.CompilerParams(vmem_limit_bytes=32 * 2**20),
        cost_estimate=pl.CostEstimate(flops=flops, bytes_accessed=moved, transcendentals=0),
    )(*operands)


def tiled(rows):
    return rows % 16 == 0


def together(*values):
    return lax.optimization_barrier(values)


def place_of(member, length):
    return jnp.where(member % 2 == 0, member // 2, length - 1 - member // 2)


def member_at(place, length):
    place = lax.rem(place + 2 * length, length)
    return jnp.where(place < length // 2, 2 * place, 2 * (length - 1 - place) + 1)


def ring_pairs(length):
    order = list(range(0, length, 2)) + list(range(length - 1, 0, -2))
    up = [(order[i], order[(i + 1) % length]) for i in range(length)]
    return up, [(b, a) for a, b in up]


def swap_pairs(length, bit):
    return [(i, i ^ bit) for i in range(length)]


def gelu_and_slope(value):
    scale = math.sqrt(2 / math.pi)
    square = value * value
    bent = jnp.tanh(scale * (value + 0.044715 * value * square))
    half = 0.5 * (1 + bent)
    slope = half + (0.5 * scale) * value * (1 - bent * bent) * (1 + 3 * 0.044715 * square)
    return value * half, slope


def rows_from(pieces, rows, length):
    full = jnp.zeros((rows * length,) + pieces[0][0].shape[1:], pieces[0][0].dtype)
    for block, member, first in pieces:
        full = lax.dynamic_update_slice(full, block, (member * rows + first, 0))
    return full


def forward_kernel(first_plan, second_plan, columns, n_row, *refs):
    n1, n2 = len(first_plan), len(second_plan)
    first_refs, second_refs = refs[:n1], refs[n1 : n1 + n2]
    inputs, wanted = refs[n1 + n2 : n1 + n2 + 2]
    away, kept, error_ref, slope_ref, second_ref = refs[n1 + n2 + 2 : n1 + n2 + 7]
    first_full, active, grad = refs[n1 + n2 + 7 :]
    tokens, width = inputs.shape
    col, row = lax.axis_index("col"), lax.axis_index("row")
    place = place_of(col, columns)
    for ref, back in zip(first_refs, first_plan):
        if back is None:
            first_full[...] = ref[...]
        else:
            rows = ref.shape[0]
            first_full[pl.ds(pl.multiple_of(member_at(place + back, columns) * rows, rows), rows), :] = ref[...]
    for ref, flips in zip(second_refs, second_plan):
        if flips is None:
            second_ref[...] = ref[...]
        else:
            rows = ref.shape[1]
            for k, flip in enumerate(flips):
                second_ref[pl.ds(pl.multiple_of((row ^ flip) * rows, rows), rows), :] = ref[k]
    pre = jnp.dot(inputs[...], first_full[...], preferred_element_type=F32)
    value, slope = gelu_and_slope(pre)
    active[...] = value.astype(BF16)
    slope_ref[...] = slope
    output = jnp.dot(active[...], second_ref[...], preferred_element_type=F32)
    error = ((output - wanted[...].astype(F32)) / tokens).astype(BF16)
    error_ref[...] = error
    grad[...] = lax.dot_general(
        active[...], error, (((0,), (0,)), ((), ())), preferred_element_type=F32
    ).astype(BF16)
    rows = width // n_row
    if tiled(rows):
        mine = row % 2
        for k in range(n_row // 2):
            for ref, side in ((away, 1 - mine), (kept, mine)):
                ref[k] = grad[pl.ds(pl.multiple_of((2 * k + side) * rows, rows), rows), :]
    else:
        away[...] = grad[: width // 2].reshape(away.shape)
        kept[...] = grad[width // 2 :].reshape(kept.shape)


def backward_kernel(columns, inputs, second_full, error, slope, *refs):
    outs, grad = refs[:-1], refs[-1]
    back = lax.dot_general(
        error[...], second_full[...], (((1,), (1,)), ((), ())), preferred_element_type=F32
    )
    grad_pre = (back * slope[...]).astype(BF16)
    value = lax.dot_general(
        inputs[...], grad_pre, (((0,), (0,)), ((), ())), preferred_element_type=F32
    )
    if len(outs) == 1:
        outs[0][...] = value.astype(BF16)
        return
    grad[...] = value
    place = place_of(lax.axis_index("col"), columns)
    rows = grad.shape[0] // columns
    half = rows // 2

    def block(away, first, count):
        start = member_at(place + away, columns) * rows + first
        return grad[pl.ds(pl.multiple_of(start, 8), count), :].astype(BF16)

    outs[0][...] = block(columns // 2, 0, half)
    outs[1][...] = block(columns // 2, half, half)
    outs[2][...] = block(0, 0, rows)
    for k in range(1, columns // 2):
        outs[2 * k + 1][...] = block(k, 0, rows)
        outs[2 * k + 2][...] = block(-k, 0, rows)


def add_kernel(ahead, forward, behind, backward, ahead_out, behind_out):
    rows, got = ahead.shape[0], forward.shape[0]
    if rows == got:
        ahead_out[...] = (ahead[...].astype(F32) + forward[...].astype(F32)).astype(BF16)
        behind_out[...] = (behind[...].astype(F32) + backward[...].astype(F32)).astype(BF16)
        return
    term = ahead[...].astype(F32)
    top = term[:got] + forward[...].astype(F32)
    ahead_out[...] = jnp.concatenate([top, term[got:]]).astype(BF16)
    term = behind[...].astype(F32)
    low = term[rows - got :] + backward[...].astype(F32)
    behind_out[...] = jnp.concatenate([term[: rows - got], low]).astype(BF16)


def add_both(ahead, forward, behind, backward):
    rows, got = ahead.shape[0], forward.shape[0]
    if tiled(rows):
        outs = [shape_of(ahead.shape)] * 2
        return call(add_kernel, outs, [], ahead, forward, behind, backward)
    zero = jnp.zeros((rows - got,) + forward.shape[1:], BF16)
    forward, backward = jnp.concatenate([forward, zero]), jnp.concatenate([zero, backward])
    return (
        (ahead.astype(F32) + forward.astype(F32)).astype(BF16),
        (behind.astype(F32) + backward.astype(F32)).astype(BF16),
    )


def first_kernel(columns, own, forward, backward, params, moment, params_out, moment_out):
    total = own[...].astype(F32) + forward[...].astype(F32) + backward[...].astype(F32)
    grad = total / columns
    moment_new = outer_momentum * moment[...] + grad
    moment_out[...] = moment_new
    params_out[...] = params[...] - outer_rate * (grad + outer_momentum * moment_new)


def halve_kernel(bit, kept, came, away_out, kept_out):
    mine = (lax.axis_index("row") // bit) % 2
    for k in range(kept_out.shape[0]):
        total = kept[2 * k + mine].astype(F32) + came[2 * k + mine].astype(F32)
        kept_out[k] = total
        other = kept[2 * k + 1 - mine].astype(F32) + came[2 * k + 1 - mine].astype(F32)
        away_out[k] = other.astype(BF16)


def per_device(hidden_in, targets, first_params, first_moment, second_params, second_moment):
    inputs, wanted = hidden_in[0, 0], targets[0, 0]
    tokens, width = inputs.shape
    columns, n_row = lax.axis_size("col"), lax.axis_size("row")
    offset = columns // 4
    rows1, rows2 = first_params.shape[1], second_params.shape[1]
    up, down = ring_pairs(columns)
    ahead_by = [(i, (i + offset) % columns) for i in range(columns)]
    last = columns // 2
    half = rows1 // 2
    place = place_of(lax.axis_index("col"), columns)
    row = lax.axis_index("row")

    own1 = first_params[0].astype(BF16)
    held = second_params[0].astype(BF16)[None]
    early_params = (second_params[0] - outer_rate * outer_momentum**2 * second_moment[0]).astype(BF16)
    early_moment = second_moment[0].astype(BF16)

    first_pieces = [(own1, 0, 0)]
    second_pieces, flips = [(held, [0])], [0]
    bit = n_row // 2
    forward = backward = own1
    for step in range(1, last + 1):
        if step == last:
            forward, backward = forward[:half], backward[half:]
        if step == EARLY_PARAMS:
            early_params, forward, backward = together(early_params, forward, backward)
        if step == EARLY_MOMENT:
            early_moment, forward, backward = together(early_moment, forward, backward)
        forward = lax.ppermute(forward, "col", up)
        backward = lax.ppermute(backward, "col", down)
        if step == EARLY_PARAMS:
            early_params = lax.ppermute(early_params, "col", ahead_by)
        if step == EARLY_MOMENT:
            early_moment = lax.ppermute(early_moment, "col", ahead_by)
        if step == last:
            break
        first_pieces += [(forward, -step, 0), (backward, step, 0)]
        while bit >= 1 and (step < last - 1 or True):
            other = lax.ppermute(held, "row", swap_pairs(n_row, bit))
            others = [f ^ bit for f in flips]
            second_pieces.append((other, others))
            flips = flips + others
            bit //= 2
            if bit >= 1:
                held = jnp.concatenate([held, other])
            break
    while bit >= 1:
        other = lax.ppermute(held, "row", swap_pairs(n_row, bit))
        others = [f ^ bit for f in flips]
        second_pieces.append((other, others))
        flips = flips + others
        bit //= 2
        if bit >= 1:
            held = jnp.concatenate([held, other])
    if tiled(rows1):
        antipode = jnp.concatenate([forward, backward])
        first_pieces.append((antipode, last, 0))
        first_plan = [p[1] for p in first_pieces]
        first_blocks = [p[0] for p in first_pieces]
    else:
        first_pieces += [(forward, last, 0), (backward, last, half)]
        placed = [(b, member_at(place + back, columns), at) for b, back, at in first_pieces]
        first_blocks, first_plan = [rows_from(placed, rows1, columns)], [None]
    if tiled(rows2):
        second_plan = [p[1] for p in second_pieces]
        second_blocks = [p[0] for p in second_pieces]
    else:
        placed = [(b[k], row ^ f, 0) for b, fs in second_pieces for k, f in enumerate(fs)]
        second_blocks, second_plan = [rows_from(placed, rows2, n_row)], [None]

    def fwd(*refs):
        forward_kernel(first_plan, second_plan, columns, n_row, *refs)

    part = shape_of((n_row // 2, rows2, width))
    away, kept, error, slope, second_full = call(
        fwd,
        [part, part, shape_of((tokens, width)), shape_of((tokens, width), F32), shape_of((width, width))],
        [pltpu.VMEM((width, width), BF16), pltpu.VMEM((tokens, width), BF16), pltpu.VMEM((width, width), BF16)],
        *first_blocks,
        *second_blocks,
        inputs,
        wanted,
        flops=6 * tokens * width * width,
    )
    if not tiled(rows2):
        pairs = jnp.concatenate([away, kept]).reshape(n_row // 2, 2, rows2, width)
        away = lax.dynamic_index_in_dim(pairs, 1 - row % 2, 1, keepdims=False)
        kept = lax.dynamic_index_in_dim(pairs, row % 2, 1, keepdims=False)
    came = lax.ppermute(away, "row", swap_pairs(n_row, 1))

    def bwd(*refs):
        backward_kernel(columns, *refs)

    block, piece = shape_of((rows1, width)), shape_of((half, width))
    outs = [piece, piece] + [block] * (columns - 1) if tiled(rows1) else [shape_of((width, width))]
    blocks = call(
        bwd,
        outs,
        [pltpu.VMEM((width, width), F32)],
        inputs,
        second_full,
        error,
        slope,
        flops=4 * tokens * width * width,
    )
    if not tiled(rows1):
        def cut(away, first=0, count=rows1):
            start = member_at(place + away, columns) * rows1 + first
            return lax.dynamic_slice_in_dim(blocks_full, start, count, 0)

        blocks_full = blocks[0]
        blocks = [cut(last, 0, half), cut(last, half, half), cut(0)]
        for k in range(1, last):
            blocks += [cut(k), cut(-k)]

    forward = lax.ppermute(blocks[0], "col", up)
    backward = lax.ppermute(blocks[1], "col", down)
    bit = 2
    grad2 = None
    for left in range(last - 1, 0, -1):
        if bit < n_row:
            if tiled(rows2):
                n = kept.shape[0] // 2
                away, kept = call(
                    lambda *refs, bit=bit: halve_kernel(bit, *refs),
                    [shape_of((n, rows2, width)), shape_of((n, rows2, width), F32)],
                    [],
                    kept,
                    came,
                )
            else:
                total = (kept.astype(F32) + came.astype(F32)).reshape(-1, 2, rows2, width)
                mine = (row // bit) % 2
                away = lax.dynamic_index_in_dim(total, 1 - mine, 1, keepdims=False).astype(BF16)
                kept = lax.dynamic_index_in_dim(total, mine, 1, keepdims=False)
            forward, backward, away = together(forward, backward, away)
            came = lax.ppermute(away, "row", swap_pairs(n_row, bit))
            bit *= 2
        elif grad2 is None:
            grad2 = ((kept[0].astype(F32) + came[0].astype(F32)) / n_row).astype(BF16)
            forward, backward, grad2 = together(forward, backward, grad2)
            grad2 = lax.ppermute(grad2, "col", ahead_by)
        forward, backward = add_both(blocks[2 * left + 1], forward, blocks[2 * left + 2], backward)
        forward = lax.ppermute(forward, "col", up)
        backward = lax.ppermute(backward, "col", down)
    if grad2 is None:
        grad2 = ((kept[0].astype(F32) + came[0].astype(F32)) / n_row).astype(BF16)
        grad2 = lax.ppermute(grad2, "col", ahead_by)

    if tiled(rows1):
        out = shape_of((rows1, width), F32)
        first_new = call(
            lambda *refs: first_kernel(columns, *refs),
            [out, out],
            [],
            blocks[2],
            forward,
            backward,
            first_params[0],
            first_moment[0],
        )
    else:
        total = blocks[2].astype(F32) + forward.astype(F32) + backward.astype(F32)
        grad = total / columns
        moment_new = outer_momentum * first_moment[0] + grad
        first_new = (first_params[0] - outer_rate * (grad + outer_momentum * moment_new), moment_new)
    grad2 = grad2.astype(F32)
    second_moment_new = outer_momentum * early_moment.astype(F32) + grad2
    second_params_new = early_params.astype(F32) - outer_rate * (1 + outer_momentum) * grad2
    return (first_new[0][None], first_new[1][None], second_params_new[None], second_moment_new[None])


EARLY_PARAMS = 4
EARLY_MOMENT = 3


def solution(mesh):
    return jax.shard_map(
        per_device,
        mesh=mesh,
        in_specs=(
            P("row", "col", None, None),
            P("row", "col", None, None),
            P("row", "col", None),
            P("row", "col", None),
            P("col", "row", None),
            P("col", "row", None),
        ),
        out_specs=(
            P("row", "col", None),
            P("row", "col", None),
            P("col", "row", None),
            P("col", "row", None),
        ),
        check_vma=False,
    )
```

```python
import math

import jax
import jax.numpy as jnp
from jax import lax
from jax.experimental import pallas as pl
from jax.experimental.pallas import tpu as pltpu
from jax.sharding import PartitionSpec as P


outer_momentum = 0.9
outer_rate = 0.7
BF16 = jnp.bfloat16
F32 = jnp.float32
WHOLE = pl.BlockSpec(memory_space=pltpu.VMEM)


def shape_of(shape, kind=BF16):
    return jax.ShapeDtypeStruct(shape, kind)


def call(kernel, outs, scratch, *operands, flops=0):
    moved = sum(o.size * o.dtype.itemsize for o in operands)
    return pl.pallas_call(
        kernel,
        out_shape=tuple(outs),
        in_specs=[WHOLE] * len(operands),
        out_specs=(WHOLE,) * len(outs),
        scratch_shapes=scratch,
        compiler_params=pltpu.CompilerParams(vmem_limit_bytes=32 * 2**20),
        cost_estimate=pl.CostEstimate(flops=flops, bytes_accessed=moved, transcendentals=0),
    )(*operands)


def tiled(rows):
    return rows % 16 == 0


def place_of(member, length):
    return jnp.where(member % 2 == 0, member // 2, length - 1 - member // 2)


def member_at(place, length):
    place = lax.rem(place + 2 * length, length)
    return jnp.where(place < length // 2, 2 * place, 2 * (length - 1 - place) + 1)


def ring_pairs(length):
    order = list(range(0, length, 2)) + list(range(length - 1, 0, -2))
    up = [(order[i], order[(i + 1) % length]) for i in range(length)]
    return up, [(b, a) for a, b in up]


def swap_pairs(length, bit):
    return [(i, i ^ bit) for i in range(length)]


def gelu_and_slope(value):
    scale = math.sqrt(2 / math.pi)
    square = value * value
    bent = jnp.tanh(scale * (value + 0.044715 * value * square))
    half = 0.5 * (1 + bent)
    slope = half + (0.5 * scale) * value * (1 - bent * bent) * (1 + 3 * 0.044715 * square)
    return value * half, slope


def rows_from(pieces, rows, length):
    full = jnp.zeros((rows * length,) + pieces[0][0].shape[1:], pieces[0][0].dtype)
    for block, member, first in pieces:
        full = lax.dynamic_update_slice(full, block, (member * rows + first, 0))
    return full


def prepare_kernel(params, moment, params_out, early_params, early_moment):
    params_out[...] = params[...].astype(BF16)
    early_params[...] = (params[...] - outer_rate * outer_momentum**2 * moment[...]).astype(BF16)
    early_moment[...] = moment[...].astype(BF16)


def forward_kernel(first_plan, second_plan, columns, n_row, *refs):
    n1, n2 = len(first_plan), len(second_plan)
    first_refs, second_refs = refs[:n1], refs[n1 : n1 + n2]
    inputs, wanted = refs[n1 + n2 : n1 + n2 + 2]
    away, kept, error_ref, slope_ref, second_ref = refs[n1 + n2 + 2 : n1 + n2 + 7]
    first_full, active, grad = refs[n1 + n2 + 7 :]
    tokens, width = inputs.shape
    col, row = lax.axis_index("col"), lax.axis_index("row")
    place = place_of(col, columns)
    for ref, back in zip(first_refs, first_plan):
        if back is None:
            first_full[...] = ref[...]
        else:
            rows = ref.shape[0]
            first_full[pl.ds(pl.multiple_of(member_at(place + back, columns) * rows, rows), rows), :] = ref[...]
    for ref, flips in zip(second_refs, second_plan):
        if flips is None:
            second_ref[...] = ref[...]
        else:
            rows = ref.shape[1]
            for k, flip in enumerate(flips):
                second_ref[pl.ds(pl.multiple_of((row ^ flip) * rows, rows), rows), :] = ref[k]
    pre = jnp.dot(inputs[...], first_full[...], preferred_element_type=F32)
    value, slope = gelu_and_slope(pre)
    active[...] = value.astype(BF16)
    slope_ref[...] = slope
    output = jnp.dot(active[...], second_ref[...], preferred_element_type=F32)
    error = ((output - wanted[...].astype(F32)) / tokens).astype(BF16)
    error_ref[...] = error
    grad[...] = lax.dot_general(
        active[...], error, (((0,), (0,)), ((), ())), preferred_element_type=F32
    ).astype(BF16)
    rows = width // n_row
    if tiled(rows):
        mine = row % 2
        for k in range(n_row // 2):
            for ref, side in ((away, 1 - mine), (kept, mine)):
                ref[k] = grad[pl.ds(pl.multiple_of((2 * k + side) * rows, rows), rows), :]
    else:
        away[...] = grad[: width // 2].reshape(away.shape)
        kept[...] = grad[width // 2 :].reshape(kept.shape)


def backward_kernel(columns, inputs, second_full, error, slope, *refs):
    outs, grad = refs[:-1], refs[-1]
    back = lax.dot_general(
        error[...], second_full[...], (((1,), (1,)), ((), ())), preferred_element_type=F32
    )
    grad_pre = (back * slope[...]).astype(BF16)
    value = lax.dot_general(
        inputs[...], grad_pre, (((0,), (0,)), ((), ())), preferred_element_type=F32
    )
    if len(outs) == 1:
        outs[0][...] = value.astype(BF16)
        return
    grad[...] = value
    place = place_of(lax.axis_index("col"), columns)
    rows = grad.shape[0] // columns
    half = rows // 2

    def block(away, first, count):
        start = member_at(place + away, columns) * rows + first
        return grad[pl.ds(pl.multiple_of(start, 8), count), :].astype(BF16)

    outs[0][...] = block(columns // 2, 0, half)
    outs[1][...] = block(columns // 2, half, half)
    outs[2][...] = block(0, 0, rows)
    for k in range(1, columns // 2):
        outs[2 * k + 1][...] = block(k, 0, rows)
        outs[2 * k + 2][...] = block(-k, 0, rows)


def add_kernel(ahead, forward, behind, backward, ahead_out, behind_out):
    rows, got = ahead.shape[0], forward.shape[0]
    if rows == got:
        ahead_out[...] = (ahead[...].astype(F32) + forward[...].astype(F32)).astype(BF16)
        behind_out[...] = (behind[...].astype(F32) + backward[...].astype(F32)).astype(BF16)
        return
    term = ahead[...].astype(F32)
    top = term[:got] + forward[...].astype(F32)
    ahead_out[...] = jnp.concatenate([top, term[got:]]).astype(BF16)
    term = behind[...].astype(F32)
    low = term[rows - got :] + backward[...].astype(F32)
    behind_out[...] = jnp.concatenate([term[: rows - got], low]).astype(BF16)


def add_both(ahead, forward, behind, backward):
    rows, got = ahead.shape[0], forward.shape[0]
    if tiled(rows):
        outs = [shape_of(ahead.shape)] * 2
        return call(add_kernel, outs, [], ahead, forward, behind, backward)
    zero = jnp.zeros((rows - got,) + forward.shape[1:], BF16)
    forward, backward = jnp.concatenate([forward, zero]), jnp.concatenate([zero, backward])
    return (
        (ahead.astype(F32) + forward.astype(F32)).astype(BF16),
        (behind.astype(F32) + backward.astype(F32)).astype(BF16),
    )


def first_kernel(columns, own, forward, backward, params, moment, params_out, moment_out):
    total = own[...].astype(F32) + forward[...].astype(F32) + backward[...].astype(F32)
    grad = total / columns
    moment_new = outer_momentum * moment[...] + grad
    moment_out[...] = moment_new
    params_out[...] = params[...] - outer_rate * (grad + outer_momentum * moment_new)


def halve_kernel(bit, kept, came, away_out, kept_out):
    mine = (lax.axis_index("row") // bit) % 2
    for k in range(kept_out.shape[0]):
        total = kept[2 * k + mine].astype(F32) + came[2 * k + mine].astype(F32)
        kept_out[k] = total
        other = kept[2 * k + 1 - mine].astype(F32) + came[2 * k + 1 - mine].astype(F32)
        away_out[k] = other.astype(BF16)


def per_device(hidden_in, targets, first_params, first_moment, second_params, second_moment):
    inputs, wanted = hidden_in[0, 0], targets[0, 0]
    tokens, width = inputs.shape
    columns, n_row = lax.axis_size("col"), lax.axis_size("row")
    offset = columns // 4
    rows1, rows2 = first_params.shape[1], second_params.shape[1]
    up, down = ring_pairs(columns)
    ahead_by = [(i, (i + offset) % columns) for i in range(columns)]
    last = columns // 2
    half = rows1 // 2
    place = place_of(lax.axis_index("col"), columns)
    row = lax.axis_index("row")

    own1 = first_params[0].astype(BF16)
    shard = shape_of((rows2, width))
    held, early_params, early_moment = call(
        prepare_kernel, [shard] * 3, [], second_params[0], second_moment[0]
    )
    held = held[None]
    first_pieces = [(own1, 0, 0)]
    forward = backward = own1
    for step in range(1, last + 1):
        if step == last:
            forward, backward = forward[:half], backward[half:]
        forward = lax.ppermute(forward, "col", up)
        backward = lax.ppermute(backward, "col", down)
        forward, backward = lax.optimization_barrier((forward, backward))
        if step < last:
            first_pieces += [(forward, -step, 0), (backward, step, 0)]
    second_pieces, flips = [(held, [0])], [0]
    bit = n_row // 2
    while bit >= 1:
        other = lax.ppermute(held, "row", swap_pairs(n_row, bit))
        others = [f ^ bit for f in flips]
        second_pieces.append((other, others))
        flips = flips + others
        bit = bit // 2
        if bit >= 1:
            held = jnp.concatenate([held, other])
    early_params = lax.ppermute(early_params, "col", ahead_by)
    early_moment = lax.ppermute(early_moment, "col", ahead_by)
    if tiled(rows1):
        antipode = jnp.concatenate([forward, backward])
        first_pieces.append((antipode, last, 0))
        first_plan = [p[1] for p in first_pieces]
        first_blocks = [p[0] for p in first_pieces]
    else:
        first_pieces += [(forward, last, 0), (backward, last, half)]
        placed = [(b, member_at(place + back, columns), at) for b, back, at in first_pieces]
        first_blocks, first_plan = [rows_from(placed, rows1, columns)], [None]
    if tiled(rows2):
        second_plan = [p[1] for p in second_pieces]
        second_blocks = [p[0] for p in second_pieces]
    else:
        placed = [(b[k], row ^ f, 0) for b, fs in second_pieces for k, f in enumerate(fs)]
        second_blocks, second_plan = [rows_from(placed, rows2, n_row)], [None]

    def fwd(*refs):
        forward_kernel(first_plan, second_plan, columns, n_row, *refs)

    part = shape_of((n_row // 2, rows2, width))
    away, kept, error, slope, second_full = call(
        fwd,
        [part, part, shape_of((tokens, width)), shape_of((tokens, width), F32), shape_of((width, width))],
        [pltpu.VMEM((width, width), BF16), pltpu.VMEM((tokens, width), BF16), pltpu.VMEM((width, width), BF16)],
        *first_blocks,
        *second_blocks,
        inputs,
        wanted,
        flops=6 * tokens * width * width,
    )
    if not tiled(rows2):
        pairs = jnp.concatenate([away, kept]).reshape(n_row // 2, 2, rows2, width)
        away = lax.dynamic_index_in_dim(pairs, 1 - row % 2, 1, keepdims=False)
        kept = lax.dynamic_index_in_dim(pairs, row % 2, 1, keepdims=False)
    came = lax.ppermute(away, "row", swap_pairs(n_row, 1))

    def bwd(*refs):
        backward_kernel(columns, *refs)

    block, piece = shape_of((rows1, width)), shape_of((half, width))
    outs = [piece, piece] + [block] * (columns - 1) if tiled(rows1) else [shape_of((width, width))]
    blocks = call(
        bwd,
        outs,
        [pltpu.VMEM((width, width), F32)],
        inputs,
        second_full,
        error,
        slope,
        flops=4 * tokens * width * width,
    )
    if not tiled(rows1):
        def cut(away, first=0, count=rows1):
            start = member_at(place + away, columns) * rows1 + first
            return lax.dynamic_slice_in_dim(blocks_full, start, count, 0)

        blocks_full = blocks[0]
        blocks = [cut(last, 0, half), cut(last, half, half), cut(0)]
        for k in range(1, last):
            blocks += [cut(k), cut(-k)]

    bit = 2
    while bit < n_row:
        if tiled(rows2):
            n = kept.shape[0] // 2
            away, kept = call(
                lambda *refs, bit=bit: halve_kernel(bit, *refs),
                [shape_of((n, rows2, width)), shape_of((n, rows2, width), F32)],
                [],
                kept,
                came,
            )
        else:
            total = (kept.astype(F32) + came.astype(F32)).reshape(-1, 2, rows2, width)
            mine = (row // bit) % 2
            away = lax.dynamic_index_in_dim(total, 1 - mine, 1, keepdims=False).astype(BF16)
            kept = lax.dynamic_index_in_dim(total, mine, 1, keepdims=False)
        came = lax.ppermute(away, "row", swap_pairs(n_row, bit))
        bit = bit * 2
    grad2 = ((kept[0].astype(F32) + came[0].astype(F32)) / n_row).astype(BF16)
    grad2 = lax.ppermute(grad2, "col", ahead_by)
    forward = lax.ppermute(blocks[0], "col", up)
    backward = lax.ppermute(blocks[1], "col", down)
    for left in range(last - 1, 0, -1):
        forward, backward = add_both(blocks[2 * left + 1], forward, blocks[2 * left + 2], backward)
        forward = lax.ppermute(forward, "col", up)
        backward = lax.ppermute(backward, "col", down)

    if tiled(rows1):
        out = shape_of((rows1, width), F32)
        first_new = call(
            lambda *refs: first_kernel(columns, *refs),
            [out, out],
            [],
            blocks[2],
            forward,
            backward,
            first_params[0],
            first_moment[0],
        )
    else:
        total = blocks[2].astype(F32) + forward.astype(F32) + backward.astype(F32)
        grad = total / columns
        moment_new = outer_momentum * first_moment[0] + grad
        first_new = (first_params[0] - outer_rate * (grad + outer_momentum * moment_new), moment_new)
    grad2 = grad2.astype(F32)
    second_moment_new = outer_momentum * early_moment.astype(F32) + grad2
    second_params_new = early_params.astype(F32) - outer_rate * (1 + outer_momentum) * grad2
    return (first_new[0][None], first_new[1][None], second_params_new[None], second_moment_new[None])


def solution(mesh):
    return jax.shard_map(
        per_device,        mesh=mesh,
        in_specs=(
            P("row", "col", None, None),
            P("row", "col", None, None),
            P("row", "col", None),
            P("row", "col", None),
            P("col", "row", None),
            P("col", "row", None),
        ),
        out_specs=(
            P("row", "col", None),
            P("row", "col", None),
            P("col", "row", None),
            P("col", "row", None),
        ),
        check_vma=False,
    )
```

```python
import math

import jax
import jax.numpy as jnp
from jax import lax
from jax.experimental import pallas as pl
from jax.experimental.pallas import tpu as pltpu
from jax.sharding import PartitionSpec as P


outer_momentum = 0.9
outer_rate = 0.7
BF16 = jnp.bfloat16
F32 = jnp.float32
AHEAD = 5
WHOLE = pl.BlockSpec(memory_space=pltpu.VMEM)


def shape_of(shape, kind=BF16):
    return jax.ShapeDtypeStruct(shape, kind)


def call(kernel, outs, scratch, *operands, flops=0):
    moved = sum(o.size * o.dtype.itemsize for o in operands)
    return pl.pallas_call(
        kernel,
        out_shape=tuple(outs),
        in_specs=[WHOLE] * len(operands),
        out_specs=(WHOLE,) * len(outs),
        scratch_shapes=scratch,
        compiler_params=pltpu.CompilerParams(vmem_limit_bytes=32 * 2**20),
        cost_estimate=pl.CostEstimate(flops=flops, bytes_accessed=moved, transcendentals=0),
    )(*operands)


def tiled(rows):
    return rows % 16 == 0


def place_of(member, length):
    return jnp.where(member % 2 == 0, member // 2, length - 1 - member // 2)


def member_at(place, length):
    place = lax.rem(place + 2 * length, length)
    return jnp.where(place < length // 2, 2 * place, 2 * (length - 1 - place) + 1)


def two_way(n_row, columns):
    order = list(range(0, columns, 2)) + list(range(columns - 1, 0, -2))
    pairs = []
    for row in range(n_row):
        for i in range(columns):
            ends = (order[i], order[(i + 1) % columns])
            source, target = ends if row % 2 == 0 else ends[::-1]
            pairs.append((row * columns + source, row * columns + target))
    return pairs


def swap_pairs(length, bit):
    return [(i, i ^ bit) for i in range(length)]


def gelu_and_slope(value):
    scale = math.sqrt(2 / math.pi)
    square = value * value
    bent = jnp.tanh(scale * (value + 0.044715 * value * square))
    half = 0.5 * (1 + bent)
    slope = half + (0.5 * scale) * value * (1 - bent * bent) * (1 + 3 * 0.044715 * square)
    return value * half, slope


def rows_from(pieces, rows, length):
    full = jnp.zeros((rows * length,) + pieces[0][0].shape[1:], pieces[0][0].dtype)
    for block, member in pieces:
        full = lax.dynamic_update_slice(full, block, (member * rows, 0))
    return full


def prepare_kernel(params, moment, early):
    ahead = early.shape[1]
    early[0] = (params[:ahead] - outer_rate * outer_momentum**2 * moment[:ahead]).astype(BF16)
    early[1] = moment[:ahead].astype(BF16)


def forward_kernel(first_plan, second_plan, columns, n_row, *refs):
    n1, n2 = len(first_plan), len(second_plan)
    first_refs, second_refs = refs[:n1], refs[n1 : n1 + n2]
    inputs, wanted = refs[n1 + n2 : n1 + n2 + 2]
    away, kept, error_ref, slope_ref, second_ref = refs[n1 + n2 + 2 : n1 + n2 + 7]
    first_full, active, grad = refs[n1 + n2 + 7 :]
    tokens, width = inputs.shape
    col, row = lax.axis_index("col"), lax.axis_index("row")
    place, way = place_of(col, columns), 1 - 2 * (row % 2)
    for ref, back in zip(first_refs, first_plan):
        if back is None:
            first_full[...] = ref[...]
        else:
            rows = ref.shape[0]
            start = member_at(place + way * back, columns) * rows
            first_full[pl.ds(pl.multiple_of(start, rows), rows), :] = ref[...]
    for ref, flips in zip(second_refs, second_plan):
        if flips is None:
            second_ref[...] = ref[...]
        else:
            rows = ref.shape[1]
            for k, flip in enumerate(flips):
                second_ref[pl.ds(pl.multiple_of((row ^ flip) * rows, rows), rows), :] = ref[k]
    pre = jnp.dot(inputs[...], first_full[...], preferred_element_type=F32)
    value, slope = gelu_and_slope(pre)
    active[...] = value.astype(BF16)
    slope_ref[...] = slope
    output = jnp.dot(active[...], second_ref[...], preferred_element_type=F32)
    error = ((output - wanted[...].astype(F32)) / tokens).astype(BF16)
    error_ref[...] = error
    grad[...] = lax.dot_general(
        active[...], error, (((0,), (0,)), ((), ())), preferred_element_type=F32
    ).astype(BF16)
    rows = width // n_row
    if tiled(rows):
        mine = row % 2
        for k in range(n_row // 2):
            for ref, side in ((away, 1 - mine), (kept, mine)):
                ref[k] = grad[pl.ds(pl.multiple_of((2 * k + side) * rows, rows), rows), :]
    else:
        away[...] = grad[: width // 2].reshape(away.shape)
        kept[...] = grad[width // 2 :].reshape(kept.shape)


def backward_kernel(columns, inputs, second_full, error, slope, *refs):
    outs, grad = refs[:-1], refs[-1]
    back = lax.dot_general(
        error[...], second_full[...], (((1,), (1,)), ((), ())), preferred_element_type=F32
    )
    grad_pre = (back * slope[...]).astype(BF16)
    value = lax.dot_general(
        inputs[...], grad_pre, (((0,), (0,)), ((), ())), preferred_element_type=F32
    )
    if len(outs) == 1:
        outs[0][...] = value.astype(BF16)
        return
    grad[...] = value.astype(BF16)
    place, way = place_of(lax.axis_index("col"), columns), 1 - 2 * (lax.axis_index("row") % 2)
    rows = grad.shape[0] // columns

    def block(away):
        start = member_at(place + way * away, columns) * rows
        return grad[pl.ds(pl.multiple_of(start, rows), rows), :]

    *own, other = outs
    for k, ref in enumerate(own):
        ref[...] = block(columns // 2 - k)
    for k in range(other.shape[0]):
        other[k] = block(-(columns // 2 - 1 - k))


def add_kernel(term, came, out):
    out[...] = (term[...].reshape(out.shape).astype(F32) + came[...].astype(F32)).astype(BF16)


def added(term, came):
    if tiled(came.shape[0]):
        return call(add_kernel, [shape_of(came.shape)], [], term, came)[0]
    return (term.reshape(came.shape).astype(F32) + came.astype(F32)).astype(BF16)


def second_kernel(n_row, ahead, kept, came, params, moment, late):
    grad = (kept[0].astype(F32) + came[0].astype(F32)) / n_row
    rows = grad.shape[0]
    late[:ahead] = grad[:ahead].astype(BF16)
    moment_new = outer_momentum * moment[ahead:] + grad[ahead:]
    params_new = params[ahead:] - outer_rate * (grad[ahead:] + outer_momentum * moment_new)
    late[ahead:rows] = params_new.astype(BF16)
    late[rows:] = moment_new.astype(BF16)


def arrive_kernel(early, late, params_out, moment_out):
    ahead, rows = early.shape[1], params_out.shape[0]
    grad = late[:ahead].astype(F32)
    params_out[:ahead] = early[0].astype(F32) - outer_rate * (1 + outer_momentum) * grad
    moment_out[:ahead] = outer_momentum * early[1].astype(F32) + grad
    params_out[ahead:] = late[ahead:rows].astype(F32)
    moment_out[ahead:] = late[rows:].astype(F32)


def first_kernel(columns, own, forward, backward, params, moment, params_out, moment_out):
    total = own[...].astype(F32) + forward[...].astype(F32) + backward[...].astype(F32)
    grad = total / columns
    moment_new = outer_momentum * moment[...] + grad
    moment_out[...] = moment_new
    params_out[...] = params[...] - outer_rate * (grad + outer_momentum * moment_new)


def halve_kernel(bit, kept, came, away_out, kept_out):
    mine = (lax.axis_index("row") // bit) % 2
    for k in range(kept_out.shape[0]):
        total = kept[2 * k + mine].astype(F32) + came[2 * k + mine].astype(F32)
        kept_out[k] = total
        other = kept[2 * k + 1 - mine].astype(F32) + came[2 * k + 1 - mine].astype(F32)
        away_out[k] = other.astype(BF16)


def per_device(hidden_in, targets, first_params, first_moment, second_params, second_moment):
    inputs, wanted = hidden_in[0, 0], targets[0, 0]
    tokens, width = inputs.shape
    columns, n_row = lax.axis_size("col"), lax.axis_size("row")
    offset = columns // 4
    rows1, rows2 = first_params.shape[1], second_params.shape[1]
    ring = two_way(n_row, columns)
    ahead_by = [(i, (i + offset) % columns) for i in range(columns)]
    last = columns // 2
    place = place_of(lax.axis_index("col"), columns)
    row = lax.axis_index("row")
    way = 1 - 2 * (row % 2)
    partner = swap_pairs(n_row, 1)

    ahead = AHEAD * rows2 // 8 // 16 * 16
    own1 = first_params[0].astype(BF16)
    held = second_params[0].astype(BF16)
    early = call(
        prepare_kernel, [shape_of((2, ahead, width))], [], second_params[0], second_moment[0]
    )[0]
    held = held[None]
    first_pieces = [(own1, 0)]
    ours, theirs = own1, lax.ppermute(own1, "row", partner)
    for step in range(1, last + 1):
        later = ours
        ours = lax.ppermute(ours, ("row", "col"), ring)
        first_pieces.append((ours, -step))
        if step < last:
            theirs = lax.ppermute(theirs, ("row", "col"), ring)
            first_pieces.append((lax.ppermute(theirs, "row", partner), step))
    second_pieces, flips = [(held, [0])], [0]
    bit = n_row // 2
    while bit >= 1:
        other = lax.ppermute(held, "row", swap_pairs(n_row, bit))
        others = [f ^ bit for f in flips]
        second_pieces.append((other, others))
        flips = flips + others
        bit = bit // 2
        if bit >= 1:
            other, _ = lax.optimization_barrier((other, later))
            held = jnp.concatenate([held, other])
    early, _ = lax.optimization_barrier((early, ours))
    early = lax.ppermute(early, "col", ahead_by)
    if tiled(rows1):
        first_blocks, first_plan = [p[0] for p in first_pieces], [p[1] for p in first_pieces]
    else:
        placed = [(b, member_at(place + way * back, columns)) for b, back in first_pieces]
        first_blocks, first_plan = [rows_from(placed, rows1, columns)], [None]
    if tiled(rows2):
        second_plan = [p[1] for p in second_pieces]
        second_blocks = [p[0] for p in second_pieces]
    else:
        placed = [(b[k], row ^ f) for b, fs in second_pieces for k, f in enumerate(fs)]
        second_blocks, second_plan = [rows_from(placed, rows2, n_row)], [None]

    def fwd(*refs):
        forward_kernel(first_plan, second_plan, columns, n_row, *refs)

    part = shape_of((n_row // 2, rows2, width))
    away, kept, error, slope, second_full = call(
        fwd,
        [part, part, shape_of((tokens, width)), shape_of((tokens, width), F32), shape_of((width, width))],
        [pltpu.VMEM((width, width), BF16), pltpu.VMEM((tokens, width), BF16), pltpu.VMEM((width, width), BF16)],
        *first_blocks,
        *second_blocks,
        inputs,
        wanted,
        flops=6 * tokens * width * width,
    )
    if not tiled(rows2):
        pairs = jnp.concatenate([away, kept]).reshape(n_row // 2, 2, rows2, width)
        away = lax.dynamic_index_in_dim(pairs, 1 - row % 2, 1, keepdims=False)
        kept = lax.dynamic_index_in_dim(pairs, row % 2, 1, keepdims=False)
    came = lax.ppermute(away, "row", swap_pairs(n_row, 1))

    def bwd(*refs):
        backward_kernel(columns, *refs)

    block = shape_of((rows1, width))
    outs = [block] * (last + 1) + [shape_of((last - 1, rows1, width))]
    outs = outs if tiled(rows1) else [shape_of((width, width))]
    blocks = call(
        bwd,
        outs,
        [pltpu.VMEM((width, width), BF16)],
        inputs,
        second_full,
        error,
        slope,
        flops=4 * tokens * width * width,
    )
    if not tiled(rows1):
        blocks_full = blocks[0]

        def cut(away):
            start = member_at(place + way * away, columns) * rows1
            return lax.dynamic_slice_in_dim(blocks_full, start, rows1, 0)

        blocks = [cut(last - k) for k in range(last + 1)]
        blocks.append(jnp.stack([cut(-(last - 1 - k)) for k in range(last - 1)]))
    *own_terms, other_terms = blocks

    bit = 2
    while bit < n_row:
        if tiled(rows2):
            n = kept.shape[0] // 2
            away, kept = call(
                lambda *refs, bit=bit: halve_kernel(bit, *refs),
                [shape_of((n, rows2, width)), shape_of((n, rows2, width), F32)],
                [],
                kept,
                came,
            )
        else:
            total = (kept.astype(F32) + came.astype(F32)).reshape(-1, 2, rows2, width)
            mine = (row // bit) % 2
            away = lax.dynamic_index_in_dim(total, 1 - mine, 1, keepdims=False).astype(BF16)
            kept = lax.dynamic_index_in_dim(total, mine, 1, keepdims=False)
        came = lax.ppermute(away, "row", swap_pairs(n_row, bit))
        bit = bit * 2
    late = call(
        lambda *refs: second_kernel(n_row, ahead, *refs),
        [shape_of((2 * rows2 - ahead, width))],
        [],
        kept,
        came,
        second_params[0],
        second_moment[0],
    )[0]
    late = lax.ppermute(late, "col", ahead_by)
    ours = lax.ppermute(own_terms[0], ("row", "col"), ring)
    other_terms = lax.ppermute(other_terms, "row", partner)
    theirs = lax.ppermute(other_terms[0], ("row", "col"), ring)
    for step in range(2, last + 1):
        ours = added(own_terms[step - 1], ours)
        ours = lax.ppermute(ours, ("row", "col"), ring)
        if step < last:
            theirs = added(other_terms[step - 1], theirs)
            theirs = lax.ppermute(theirs, ("row", "col"), ring)
    theirs = lax.ppermute(theirs, "row", partner)

    if tiled(rows1):
        out = shape_of((rows1, width), F32)
        first_new = call(
            lambda *refs: first_kernel(columns, *refs),
            [out, out],
            [],
            own_terms[last],
            ours,
            theirs,
            first_params[0],
            first_moment[0],
        )
    else:
        total = own_terms[last].astype(F32) + ours.astype(F32) + theirs.astype(F32)
        grad = total / columns
        moment_new = outer_momentum * first_moment[0] + grad
        first_new = (first_params[0] - outer_rate * (grad + outer_momentum * moment_new), moment_new)
    second_new = call(arrive_kernel, [shape_of((rows2, width), F32)] * 2, [], early, late)
    return (first_new[0][None], first_new[1][None], second_new[0][None], second_new[1][None])


def solution(mesh):
    return jax.shard_map(
        per_device,        mesh=mesh,
        in_specs=(
            P("row", "col", None, None),
            P("row", "col", None, None),
            P("row", "col", None),
            P("row", "col", None),
            P("col", "row", None),
            P("col", "row", None),
        ),
        out_specs=(
            P("row", "col", None),
            P("row", "col", None),
            P("col", "row", None),
            P("col", "row", None),
        ),
        check_vma=False,
    )
```

```python
import math

import jax
import jax.numpy as jnp
from jax import lax
from jax.experimental import pallas as pl
from jax.experimental.pallas import tpu as pltpu
from jax.sharding import PartitionSpec as P


outer_momentum = 0.9
outer_rate = 0.7
BF16 = jnp.bfloat16
F32 = jnp.float32
AHEAD = 9
WHOLE = pl.BlockSpec(memory_space=pltpu.VMEM)


def shape_of(shape, kind=BF16):
    return jax.ShapeDtypeStruct(shape, kind)


def call(kernel, outs, scratch, *operands, flops=0):
    moved = sum(o.size * o.dtype.itemsize for o in operands)
    return pl.pallas_call(
        kernel,
        out_shape=tuple(outs),
        in_specs=[WHOLE] * len(operands),
        out_specs=(WHOLE,) * len(outs),
        scratch_shapes=scratch,
        compiler_params=pltpu.CompilerParams(vmem_limit_bytes=32 * 2**20),
        cost_estimate=pl.CostEstimate(flops=flops, bytes_accessed=moved, transcendentals=0),
    )(*operands)


def tiled(rows):
    return rows % 16 == 0


def place_of(member, length):
    return jnp.where(member % 2 == 0, member // 2, length - 1 - member // 2)


def member_at(place, length):
    place = lax.rem(place + 2 * length, length)
    return jnp.where(place < length // 2, 2 * place, 2 * (length - 1 - place) + 1)


def two_way(n_row, columns):
    order = list(range(0, columns, 2)) + list(range(columns - 1, 0, -2))
    pairs = []
    for row in range(n_row):
        for i in range(columns):
            ends = (order[i], order[(i + 1) % columns])
            source, target = ends if row % 2 == 0 else ends[::-1]
            pairs.append((row * columns + source, row * columns + target))
    return pairs


def swap_pairs(length, bit):
    return [(i, i ^ bit) for i in range(length)]


def gelu_and_slope(value):
    scale = math.sqrt(2 / math.pi)
    square = value * value
    bent = jnp.tanh(scale * (value + 0.044715 * value * square))
    half = 0.5 * (1 + bent)
    slope = half + (0.5 * scale) * value * (1 - bent * bent) * (1 + 3 * 0.044715 * square)
    return value * half, slope


def rows_from(pieces, rows, length):
    full = jnp.zeros((rows * length,) + pieces[0][0].shape[1:], pieces[0][0].dtype)
    for block, member in pieces:
        full = lax.dynamic_update_slice(full, block, (member * rows, 0))
    return full


def prepare_kernel(params, moment, early):
    ahead = early.shape[1]
    early[0] = (params[:ahead] - outer_rate * outer_momentum**2 * moment[:ahead]).astype(BF16)
    early[1] = moment[:ahead].astype(BF16)


def forward_kernel(first_plan, second_plan, columns, n_row, *refs):
    n1, n2 = len(first_plan), len(second_plan)
    first_refs, second_refs = refs[:n1], refs[n1 : n1 + n2]
    inputs, wanted = refs[n1 + n2 : n1 + n2 + 2]
    away, kept, error_ref, slope_ref, second_ref = refs[n1 + n2 + 2 : n1 + n2 + 7]
    first_full, active, grad = refs[n1 + n2 + 7 :]
    tokens, width = inputs.shape
    col, row = lax.axis_index("col"), lax.axis_index("row")
    place, way = place_of(col, columns), 1 - 2 * (row % 2)
    for ref, back in zip(first_refs, first_plan):
        if back is None:
            first_full[...] = ref[...]
        else:
            rows = ref.shape[0]
            start = member_at(place + way * back, columns) * rows
            first_full[pl.ds(pl.multiple_of(start, rows), rows), :] = ref[...]
    for ref, flips in zip(second_refs, second_plan):
        if flips is None:
            second_ref[...] = ref[...]
        else:
            rows = ref.shape[1]
            for k, flip in enumerate(flips):
                second_ref[pl.ds(pl.multiple_of((row ^ flip) * rows, rows), rows), :] = ref[k]
    pre = jnp.dot(inputs[...], first_full[...], preferred_element_type=F32)
    value, slope = gelu_and_slope(pre)
    active[...] = value.astype(BF16)
    slope_ref[...] = slope
    output = jnp.dot(active[...], second_ref[...], preferred_element_type=F32)
    error = ((output - wanted[...].astype(F32)) / tokens).astype(BF16)
    error_ref[...] = error
    grad[...] = lax.dot_general(
        active[...], error, (((0,), (0,)), ((), ())), preferred_element_type=F32
    ).astype(BF16)
    rows = width // n_row
    if tiled(rows):
        mine = row % 2
        for k in range(n_row // 2):
            for ref, side in ((away, 1 - mine), (kept, mine)):
                ref[k] = grad[pl.ds(pl.multiple_of((2 * k + side) * rows, rows), rows), :]
    else:
        away[...] = grad[: width // 2].reshape(away.shape)
        kept[...] = grad[width // 2 :].reshape(kept.shape)


def backward_kernel(columns, inputs, second_full, error, slope, *refs):
    outs, grad = refs[:-1], refs[-1]
    back = lax.dot_general(
        error[...], second_full[...], (((1,), (1,)), ((), ())), preferred_element_type=F32
    )
    grad_pre = (back * slope[...]).astype(BF16)
    value = lax.dot_general(
        inputs[...], grad_pre, (((0,), (0,)), ((), ())), preferred_element_type=F32
    )
    if len(outs) == 1:
        outs[0][...] = value.astype(BF16)
        return
    grad[...] = value.astype(BF16)
    place, way = place_of(lax.axis_index("col"), columns), 1 - 2 * (lax.axis_index("row") % 2)
    rows = grad.shape[0] // columns

    def block(away):
        start = member_at(place + way * away, columns) * rows
        return grad[pl.ds(pl.multiple_of(start, rows), rows), :]

    *own, other = outs
    for k, ref in enumerate(own):
        ref[...] = block(columns // 2 - k)
    for k in range(other.shape[0]):
        other[k] = block(-(columns // 2 - 1 - k))


def add_kernel(term, came, out):
    out[...] = (term[...].reshape(out.shape).astype(F32) + came[...].astype(F32)).astype(BF16)


def added(term, came):
    if tiled(came.shape[0]):
        return call(add_kernel, [shape_of(came.shape)], [], term, came)[0]
    return (term.reshape(came.shape).astype(F32) + came.astype(F32)).astype(BF16)


def second_kernel(n_row, ahead, kept, came, params, moment, late):
    grad = (kept[0].astype(F32) + came[0].astype(F32)) / n_row
    rows = grad.shape[0]
    late[:ahead] = grad[:ahead].astype(BF16)
    moment_new = outer_momentum * moment[ahead:] + grad[ahead:]
    params_new = params[ahead:] - outer_rate * (grad[ahead:] + outer_momentum * moment_new)
    late[ahead:rows] = params_new.astype(BF16)
    late[rows:] = moment_new.astype(BF16)


def closing_kernel(columns, own, ours, theirs, params, moment, early, late, *outs):
    params_out, moment_out, second_params, second_moment = outs
    ahead, rows = early.shape[1], second_params.shape[0]
    grad = late[:ahead].astype(F32)
    second_params[:ahead] = early[0].astype(F32) - outer_rate * (1 + outer_momentum) * grad
    second_moment[:ahead] = outer_momentum * early[1].astype(F32) + grad
    second_params[ahead:] = late[ahead:rows].astype(F32)
    second_moment[ahead:] = late[rows:].astype(F32)
    grad = (own[...].astype(F32) + ours[...].astype(F32) + theirs[...].astype(F32)) / columns
    moment_new = outer_momentum * moment[...] + grad
    moment_out[...] = moment_new
    params_out[...] = params[...] - outer_rate * (grad + outer_momentum * moment_new)


def halve_kernel(bit, kept, came, away_out, kept_out):
    mine = (lax.axis_index("row") // bit) % 2
    for k in range(kept_out.shape[0]):
        total = kept[2 * k + mine].astype(F32) + came[2 * k + mine].astype(F32)
        kept_out[k] = total
        other = kept[2 * k + 1 - mine].astype(F32) + came[2 * k + 1 - mine].astype(F32)
        away_out[k] = other.astype(BF16)


def per_device(hidden_in, targets, first_params, first_moment, second_params, second_moment):
    inputs, wanted = hidden_in[0, 0], targets[0, 0]
    tokens, width = inputs.shape
    columns, n_row = lax.axis_size("col"), lax.axis_size("row")
    offset = columns // 4
    rows1, rows2 = first_params.shape[1], second_params.shape[1]
    ring = two_way(n_row, columns)
    ahead_by = [(i, (i + offset) % columns) for i in range(columns)]
    last = columns // 2
    place = place_of(lax.axis_index("col"), columns)
    row = lax.axis_index("row")
    way = 1 - 2 * (row % 2)
    partner = swap_pairs(n_row, 1)

    ahead = AHEAD * rows2 // 14 // 16 * 16
    own1 = first_params[0].astype(BF16)
    held = second_params[0].astype(BF16)
    early = call(
        prepare_kernel, [shape_of((2, ahead, width))], [], second_params[0], second_moment[0]
    )[0]
    held = held[None]
    first_pieces = [(own1, 0)]
    ours, theirs = own1, lax.ppermute(own1, "row", partner)
    for step in range(1, last + 1):
        later = ours
        ours = lax.ppermute(ours, ("row", "col"), ring)
        first_pieces.append((ours, -step))
        if step < last:
            theirs = lax.ppermute(theirs, ("row", "col"), ring)
            first_pieces.append((lax.ppermute(theirs, "row", partner), step))
    second_pieces, flips = [(held, [0])], [0]
    bit = n_row // 2
    while bit >= 1:
        other = lax.ppermute(held, "row", swap_pairs(n_row, bit))
        others = [f ^ bit for f in flips]
        second_pieces.append((other, others))
        flips = flips + others
        bit = bit // 2
        if bit >= 1:
            other, _ = lax.optimization_barrier((other, later))
            held = jnp.concatenate([held, other])
    early, _ = lax.optimization_barrier((early, ours))
    early = lax.ppermute(early, "col", ahead_by)
    if tiled(rows1):
        first_blocks, first_plan = [p[0] for p in first_pieces], [p[1] for p in first_pieces]
    else:
        placed = [(b, member_at(place + way * back, columns)) for b, back in first_pieces]
        first_blocks, first_plan = [rows_from(placed, rows1, columns)], [None]
    if tiled(rows2):
        second_plan = [p[1] for p in second_pieces]
        second_blocks = [p[0] for p in second_pieces]
    else:
        placed = [(b[k], row ^ f) for b, fs in second_pieces for k, f in enumerate(fs)]
        second_blocks, second_plan = [rows_from(placed, rows2, n_row)], [None]

    def fwd(*refs):
        forward_kernel(first_plan, second_plan, columns, n_row, *refs)

    part = shape_of((n_row // 2, rows2, width))
    away, kept, error, slope, second_full = call(
        fwd,
        [part, part, shape_of((tokens, width)), shape_of((tokens, width), F32), shape_of((width, width))],
        [pltpu.VMEM((width, width), BF16), pltpu.VMEM((tokens, width), BF16), pltpu.VMEM((width, width), BF16)],
        *first_blocks,
        *second_blocks,
        inputs,
        wanted,
        flops=6 * tokens * width * width,
    )
    if not tiled(rows2):
        pairs = jnp.concatenate([away, kept]).reshape(n_row // 2, 2, rows2, width)
        away = lax.dynamic_index_in_dim(pairs, 1 - row % 2, 1, keepdims=False)
        kept = lax.dynamic_index_in_dim(pairs, row % 2, 1, keepdims=False)
    came = lax.ppermute(away, "row", swap_pairs(n_row, 1))

    def bwd(*refs):
        backward_kernel(columns, *refs)

    block = shape_of((rows1, width))
    outs = [block] * (last + 1) + [shape_of((last - 1, rows1, width))]
    outs = outs if tiled(rows1) else [shape_of((width, width))]
    blocks = call(
        bwd,
        outs,
        [pltpu.VMEM((width, width), BF16)],
        inputs,
        second_full,
        error,
        slope,
        flops=4 * tokens * width * width,
    )
    if not tiled(rows1):
        blocks_full = blocks[0]

        def cut(away):
            start = member_at(place + way * away, columns) * rows1
            return lax.dynamic_slice_in_dim(blocks_full, start, rows1, 0)

        blocks = [cut(last - k) for k in range(last + 1)]
        blocks.append(jnp.stack([cut(-(last - 1 - k)) for k in range(last - 1)]))
    *own_terms, other_terms = blocks

    bit = 2
    while bit < n_row:
        if tiled(rows2):
            n = kept.shape[0] // 2
            away, kept = call(
                lambda *refs, bit=bit: halve_kernel(bit, *refs),
                [shape_of((n, rows2, width)), shape_of((n, rows2, width), F32)],
                [],
                kept,
                came,
            )
        else:
            total = (kept.astype(F32) + came.astype(F32)).reshape(-1, 2, rows2, width)
            mine = (row // bit) % 2
            away = lax.dynamic_index_in_dim(total, 1 - mine, 1, keepdims=False).astype(BF16)
            kept = lax.dynamic_index_in_dim(total, mine, 1, keepdims=False)
        came = lax.ppermute(away, "row", swap_pairs(n_row, bit))
        bit = bit * 2
    late = call(
        lambda *refs: second_kernel(n_row, ahead, *refs),
        [shape_of((2 * rows2 - ahead, width))],
        [],
        kept,
        came,
        second_params[0],
        second_moment[0],
    )[0]
    late = lax.ppermute(late, "col", ahead_by)
    ours = lax.ppermute(own_terms[0], ("row", "col"), ring)
    other_terms = lax.ppermute(other_terms, "row", partner)
    theirs = lax.ppermute(other_terms[0], ("row", "col"), ring)
    for step in range(2, last + 1):
        ours = added(own_terms[step - 1], ours)
        ours = lax.ppermute(ours, ("row", "col"), ring)
        if step < last:
            theirs = added(other_terms[step - 1], theirs)
            theirs = lax.ppermute(theirs, ("row", "col"), ring)
    theirs = lax.ppermute(theirs, "row", partner)

    news = call(
        lambda *refs: closing_kernel(columns, *refs),
        [shape_of((rows1, width), F32)] * 2 + [shape_of((rows2, width), F32)] * 2,
        [],
        own_terms[last],
        ours,
        theirs,
        first_params[0],
        first_moment[0],
        early,
        late,
    )
    return tuple(new[None] for new in news)


def solution(mesh):
    return jax.shard_map(
        per_device,        mesh=mesh,
        in_specs=(
            P("row", "col", None, None),
            P("row", "col", None, None),
            P("row", "col", None),
            P("row", "col", None),
            P("col", "row", None),
            P("col", "row", None),
        ),
        out_specs=(
            P("row", "col", None),
            P("row", "col", None),
            P("col", "row", None),
            P("col", "row", None),
        ),
        check_vma=False,
    )
```

```python
import math

import jax
import jax.numpy as jnp
from jax import lax
from jax.experimental import pallas as pl
from jax.experimental.pallas import tpu as pltpu
from jax.sharding import PartitionSpec as P


outer_momentum = 0.9
outer_rate = 0.7
BF16 = jnp.bfloat16
F32 = jnp.float32
AHEAD = 8
WHOLE = pl.BlockSpec(memory_space=pltpu.VMEM)


def shape_of(shape, kind=BF16):
    return jax.ShapeDtypeStruct(shape, kind)


def call(kernel, outs, scratch, *operands, flops=0):
    moved = sum(o.size * o.dtype.itemsize for o in operands)
    return pl.pallas_call(
        kernel,
        out_shape=tuple(outs),
        in_specs=[WHOLE] * len(operands),
        out_specs=(WHOLE,) * len(outs),
        scratch_shapes=scratch,
        compiler_params=pltpu.CompilerParams(vmem_limit_bytes=32 * 2**20),
        cost_estimate=pl.CostEstimate(flops=flops, bytes_accessed=moved, transcendentals=0),
    )(*operands)


def tiled(rows):
    return rows % 16 == 0


def place_of(member, length):
    return jnp.where(member % 2 == 0, member // 2, length - 1 - member // 2)


def member_at(place, length):
    place = lax.rem(place + 2 * length, length)
    return jnp.where(place < length // 2, 2 * place, 2 * (length - 1 - place) + 1)


def two_way(n_row, columns):
    order = list(range(0, columns, 2)) + list(range(columns - 1, 0, -2))
    pairs = []
    for row in range(n_row):
        for i in range(columns):
            ends = (order[i], order[(i + 1) % columns])
            source, target = ends if row % 2 == 0 else ends[::-1]
            pairs.append((row * columns + source, row * columns + target))
    return pairs


def swap_pairs(length, bit):
    return [(i, i ^ bit) for i in range(length)]


def gelu_and_slope(value):
    scale = math.sqrt(2 / math.pi)
    square = value * value
    bent = jnp.tanh(scale * (value + 0.044715 * value * square))
    half = 0.5 * (1 + bent)
    slope = half + (0.5 * scale) * value * (1 - bent * bent) * (1 + 3 * 0.044715 * square)
    return value * half, slope


def rows_from(pieces, rows, length):
    full = jnp.zeros((rows * length,) + pieces[0][0].shape[1:], pieces[0][0].dtype)
    for block, member in pieces:
        full = lax.dynamic_update_slice(full, block, (member * rows, 0))
    return full


def prepare_kernel(params, moment, early):
    ahead = early.shape[1]
    early[0] = (params[:ahead] - outer_rate * outer_momentum**2 * moment[:ahead]).astype(BF16)
    early[1] = moment[:ahead].astype(BF16)


def forward_kernel(first_plan, second_plan, columns, n_row, *refs):
    n1, n2 = len(first_plan), len(second_plan)
    first_refs, second_refs = refs[:n1], refs[n1 : n1 + n2]
    inputs, wanted = refs[n1 + n2 : n1 + n2 + 2]
    away, kept, error_ref, slope_ref, second_ref = refs[n1 + n2 + 2 : n1 + n2 + 7]
    first_full, active, grad = refs[n1 + n2 + 7 :]
    tokens, width = inputs.shape
    col, row = lax.axis_index("col"), lax.axis_index("row")
    place, way = place_of(col, columns), 1 - 2 * (row % 2)
    for ref, back in zip(first_refs, first_plan):
        if back is None:
            first_full[...] = ref[...]
        else:
            rows = ref.shape[0]
            start = member_at(place + way * back, columns) * rows
            first_full[pl.ds(pl.multiple_of(start, rows), rows), :] = ref[...]
    for ref, flips in zip(second_refs, second_plan):
        if flips is None:
            second_ref[...] = ref[...]
        else:
            rows = ref.shape[1]
            for k, flip in enumerate(flips):
                second_ref[pl.ds(pl.multiple_of((row ^ flip) * rows, rows), rows), :] = ref[k]
    cut = width // 2 // 128 * 128
    output = 0.0
    for some in (slice(0, cut), slice(cut, width)):
        pre = jnp.dot(inputs[...], first_full[:, some], preferred_element_type=F32)
        value, slope = gelu_and_slope(pre)
        active[:, some] = value.astype(BF16)
        slope_ref[:, some] = slope
        output += jnp.dot(active[:, some], second_ref[some, :], preferred_element_type=F32)
    error = ((output - wanted[...].astype(F32)) / tokens).astype(BF16)
    error_ref[...] = error
    grad[...] = lax.dot_general(
        active[...], error, (((0,), (0,)), ((), ())), preferred_element_type=F32
    ).astype(BF16)
    rows = width // n_row
    if tiled(rows):
        mine = row % 2
        for k in range(n_row // 2):
            for ref, side in ((away, 1 - mine), (kept, mine)):
                ref[k] = grad[pl.ds(pl.multiple_of((2 * k + side) * rows, rows), rows), :]
    else:
        away[...] = grad[: width // 2].reshape(away.shape)
        kept[...] = grad[width // 2 :].reshape(kept.shape)


def backward_kernel(columns, inputs, second_full, error, slope, *refs):
    outs, grad = refs[:-1], refs[-1]
    back = lax.dot_general(
        error[...], second_full[...], (((1,), (1,)), ((), ())), preferred_element_type=F32
    )
    grad_pre = (back * slope[...]).astype(BF16)
    value = lax.dot_general(
        inputs[...], grad_pre, (((0,), (0,)), ((), ())), preferred_element_type=F32
    )
    if len(outs) == 1:
        outs[0][...] = value.astype(BF16)
        return
    grad[...] = value.astype(BF16)
    place, way = place_of(lax.axis_index("col"), columns), 1 - 2 * (lax.axis_index("row") % 2)
    rows = grad.shape[0] // columns

    def block(away):
        start = member_at(place + way * away, columns) * rows
        return grad[pl.ds(pl.multiple_of(start, rows), rows), :]

    *own, other = outs
    for k, ref in enumerate(own):
        ref[...] = block(columns // 2 - k)
    for k in range(other.shape[0]):
        other[k] = block(-(columns // 2 - 1 - k))


def add_kernel(term, came, out):
    out[...] = (term[...].reshape(out.shape).astype(F32) + came[...].astype(F32)).astype(BF16)


def added(term, came):
    if tiled(came.shape[0]):
        return call(add_kernel, [shape_of(came.shape)], [], term, came)[0]
    return (term.reshape(came.shape).astype(F32) + came.astype(F32)).astype(BF16)


def second_kernel(n_row, ahead, kept, came, params, moment, late):
    grad = (kept[0].astype(F32) + came[0].astype(F32)) / n_row
    rows = grad.shape[0]
    late[:ahead] = grad[:ahead].astype(BF16)
    moment_new = outer_momentum * moment[ahead:] + grad[ahead:]
    params_new = params[ahead:] - outer_rate * (grad[ahead:] + outer_momentum * moment_new)
    late[ahead:rows] = params_new.astype(BF16)
    late[rows:] = moment_new.astype(BF16)


def arrive_kernel(early, late, params_out, moment_out):
    ahead, rows = early.shape[1], params_out.shape[0]
    grad = late[:ahead].astype(F32)
    params_out[:ahead] = early[0].astype(F32) - outer_rate * (1 + outer_momentum) * grad
    moment_out[:ahead] = outer_momentum * early[1].astype(F32) + grad
    params_out[ahead:] = late[ahead:rows].astype(F32)
    moment_out[ahead:] = late[rows:].astype(F32)


def closing_kernel(columns, own, ours, theirs, params, moment, params_out, moment_out):
    grad = (own[...].astype(F32) + ours[...].astype(F32) + theirs[...].astype(F32)) / columns
    moment_new = outer_momentum * moment[...] + grad
    moment_out[...] = moment_new
    params_out[...] = params[...] - outer_rate * (grad + outer_momentum * moment_new)


def halve_kernel(bit, kept, came, away_out, kept_out):
    mine = (lax.axis_index("row") // bit) % 2
    for k in range(kept_out.shape[0]):
        total = kept[2 * k + mine].astype(F32) + came[2 * k + mine].astype(F32)
        kept_out[k] = total
        other = kept[2 * k + 1 - mine].astype(F32) + came[2 * k + 1 - mine].astype(F32)
        away_out[k] = other.astype(BF16)


def per_device(hidden_in, targets, first_params, first_moment, second_params, second_moment):
    inputs, wanted = hidden_in[0, 0], targets[0, 0]
    tokens, width = inputs.shape
    columns, n_row = lax.axis_size("col"), lax.axis_size("row")
    offset = columns // 4
    rows1, rows2 = first_params.shape[1], second_params.shape[1]
    ring = two_way(n_row, columns)
    ahead_by = [(i, (i + offset) % columns) for i in range(columns)]
    last = columns // 2
    place = place_of(lax.axis_index("col"), columns)
    row = lax.axis_index("row")
    way = 1 - 2 * (row % 2)
    partner = swap_pairs(n_row, 1)

    ahead = AHEAD * rows2 // 14 // 16 * 16
    own1 = first_params[0].astype(BF16)
    held = second_params[0].astype(BF16)
    early = call(
        prepare_kernel, [shape_of((2, ahead, width))], [], second_params[0], second_moment[0]
    )[0]
    held = held[None]
    first_pieces = [(own1, 0)]
    ours, theirs = own1, lax.ppermute(own1, "row", partner)
    for step in range(1, last + 1):
        later = ours
        ours = lax.ppermute(ours, ("row", "col"), ring)
        first_pieces.append((ours, -step))
        if step < last:
            theirs = lax.ppermute(theirs, ("row", "col"), ring)
            across = lax.ppermute(theirs, "row", partner)
            first_pieces.append((across, step))
    second_pieces, flips = [(held, [0])], [0]
    bit = n_row // 2
    while bit >= 1:
        other = lax.ppermute(held, "row", swap_pairs(n_row, bit))
        others = [f ^ bit for f in flips]
        second_pieces.append((other, others))
        flips = flips + others
        bit = bit // 2
        if bit >= 1:
            other, _ = lax.optimization_barrier((other, later))
            held = jnp.concatenate([held, other])
    early, _ = lax.optimization_barrier((early, theirs))
    early = lax.ppermute(early, "col", ahead_by)
    if tiled(rows1):
        first_blocks, first_plan = [p[0] for p in first_pieces], [p[1] for p in first_pieces]
    else:
        placed = [(b, member_at(place + way * back, columns)) for b, back in first_pieces]
        first_blocks, first_plan = [rows_from(placed, rows1, columns)], [None]
    if tiled(rows2):
        second_plan = [p[1] for p in second_pieces]
        second_blocks = [p[0] for p in second_pieces]
    else:
        placed = [(b[k], row ^ f) for b, fs in second_pieces for k, f in enumerate(fs)]
        second_blocks, second_plan = [rows_from(placed, rows2, n_row)], [None]

    def fwd(*refs):
        forward_kernel(first_plan, second_plan, columns, n_row, *refs)

    part = shape_of((n_row // 2, rows2, width))
    away, kept, error, slope, second_full = call(
        fwd,
        [part, part, shape_of((tokens, width)), shape_of((tokens, width), F32), shape_of((width, width))],
        [pltpu.VMEM((width, width), BF16), pltpu.VMEM((tokens, width), BF16), pltpu.VMEM((width, width), BF16)],
        *first_blocks,
        *second_blocks,
        inputs,
        wanted,
        flops=6 * tokens * width * width,
    )
    if not tiled(rows2):
        pairs = jnp.concatenate([away, kept]).reshape(n_row // 2, 2, rows2, width)
        away = lax.dynamic_index_in_dim(pairs, 1 - row % 2, 1, keepdims=False)
        kept = lax.dynamic_index_in_dim(pairs, row % 2, 1, keepdims=False)
    came = lax.ppermute(away, "row", swap_pairs(n_row, 1))

    def bwd(*refs):
        backward_kernel(columns, *refs)

    block = shape_of((rows1, width))
    outs = [block] * (last + 1) + [shape_of((last - 1, rows1, width))]
    outs = outs if tiled(rows1) else [shape_of((width, width))]
    blocks = call(
        bwd,
        outs,
        [pltpu.VMEM((width, width), BF16)],
        inputs,
        second_full,
        error,
        slope,
        flops=4 * tokens * width * width,
    )
    if not tiled(rows1):
        blocks_full = blocks[0]

        def cut(away):
            start = member_at(place + way * away, columns) * rows1
            return lax.dynamic_slice_in_dim(blocks_full, start, rows1, 0)

        blocks = [cut(last - k) for k in range(last + 1)]
        blocks.append(jnp.stack([cut(-(last - 1 - k)) for k in range(last - 1)]))
    *own_terms, other_terms = blocks

    bit = 2
    while bit < n_row:
        if tiled(rows2):
            n = kept.shape[0] // 2
            away, kept = call(
                lambda *refs, bit=bit: halve_kernel(bit, *refs),
                [shape_of((n, rows2, width)), shape_of((n, rows2, width), F32)],
                [],
                kept,
                came,
            )
        else:
            total = (kept.astype(F32) + came.astype(F32)).reshape(-1, 2, rows2, width)
            mine = (row // bit) % 2
            away = lax.dynamic_index_in_dim(total, 1 - mine, 1, keepdims=False).astype(BF16)
            kept = lax.dynamic_index_in_dim(total, mine, 1, keepdims=False)
        came = lax.ppermute(away, "row", swap_pairs(n_row, bit))
        bit = bit * 2
    late = call(
        lambda *refs: second_kernel(n_row, ahead, *refs),
        [shape_of((2 * rows2 - ahead, width))],
        [],
        kept,
        came,
        second_params[0],
        second_moment[0],
    )[0]
    late = lax.ppermute(late, "col", ahead_by)
    ours = lax.ppermute(own_terms[0], ("row", "col"), ring)
    other_terms = lax.ppermute(other_terms, "row", partner)
    theirs = lax.ppermute(other_terms[0], ("row", "col"), ring)
    for step in range(2, last + 1):
        ours = added(own_terms[step - 1], ours)
        ours = lax.ppermute(ours, ("row", "col"), ring)
        if step < last:
            theirs = added(other_terms[step - 1], theirs)
            theirs = lax.ppermute(theirs, ("row", "col"), ring)
    theirs = lax.ppermute(theirs, "row", partner)

    second_new = call(arrive_kernel, [shape_of((rows2, width), F32)] * 2, [], early, late)
    first_new = call(
        lambda *refs: closing_kernel(columns, *refs),
        [shape_of((rows1, width), F32)] * 2,
        [],
        own_terms[last],
        ours,
        theirs,
        first_params[0],
        first_moment[0],
    )
    return tuple(new[None] for new in (*first_new, *second_new))


def solution(mesh):
    return jax.shard_map(
        per_device,        mesh=mesh,
        in_specs=(
            P("row", "col", None, None),
            P("row", "col", None, None),
            P("row", "col", None),
            P("row", "col", None),
            P("col", "row", None),
            P("col", "row", None),
        ),
        out_specs=(
            P("row", "col", None),
            P("row", "col", None),
            P("col", "row", None),
            P("col", "row", None),
        ),
        check_vma=False,
    )
```

```python
import math

import jax
import jax.numpy as jnp
from jax import lax
from jax.experimental import pallas as pl
from jax.experimental.pallas import tpu as pltpu
from jax.sharding import PartitionSpec as P


outer_momentum = 0.9
outer_rate = 0.7
BF16 = jnp.bfloat16
F32 = jnp.float32
AHEAD = 8
WHOLE = pl.BlockSpec(memory_space=pltpu.VMEM)


def shape_of(shape, kind=BF16):
    return jax.ShapeDtypeStruct(shape, kind)


def call(kernel, outs, scratch, *operands, flops=0):
    moved = sum(o.size * o.dtype.itemsize for o in operands)
    return pl.pallas_call(
        kernel,
        out_shape=tuple(outs),
        in_specs=[WHOLE] * len(operands),
        out_specs=(WHOLE,) * len(outs),
        scratch_shapes=scratch,
        compiler_params=pltpu.CompilerParams(vmem_limit_bytes=32 * 2**20),
        cost_estimate=pl.CostEstimate(flops=flops, bytes_accessed=moved, transcendentals=0),
    )(*operands)


def tiled(rows):
    return rows % 16 == 0


def place_of(member, length):
    return jnp.where(member % 2 == 0, member // 2, length - 1 - member // 2)


def member_at(place, length):
    place = lax.rem(place + 2 * length, length)
    return jnp.where(place < length // 2, 2 * place, 2 * (length - 1 - place) + 1)


def two_way(n_row, columns):
    order = list(range(0, columns, 2)) + list(range(columns - 1, 0, -2))
    pairs = []
    for row in range(n_row):
        for i in range(columns):
            ends = (order[i], order[(i + 1) % columns])
            source, target = ends if row % 2 == 0 else ends[::-1]
            pairs.append((row * columns + source, row * columns + target))
    return pairs


def swap_pairs(length, bit):
    return [(i, i ^ bit) for i in range(length)]


def gelu_and_slope(value):
    scale = math.sqrt(2 / math.pi)
    square = value * value
    half = 0.5 + 0.5 * jnp.tanh(value * (scale + scale * 0.044715 * square))
    result = value * half
    slope = half + (result - result * half) * (2 * scale + 6 * scale * 0.044715 * square)
    return result, slope


def rows_from(pieces, rows, length):
    full = jnp.zeros((rows * length,) + pieces[0][0].shape[1:], pieces[0][0].dtype)
    for block, member in pieces:
        full = lax.dynamic_update_slice(full, block, (member * rows, 0))
    return full


def prepare_kernel(params, moment, early):
    ahead = early.shape[1]
    early[0] = (params[:ahead] - outer_rate * outer_momentum**2 * moment[:ahead]).astype(BF16)
    early[1] = moment[:ahead].astype(BF16)


def forward_kernel(first_plan, second_plan, columns, n_row, *refs):
    n1, n2 = len(first_plan), len(second_plan)
    first_refs, second_refs = refs[:n1], refs[n1 : n1 + n2]
    inputs, wanted = refs[n1 + n2 : n1 + n2 + 2]
    away, kept, error_ref, slope_ref, second_ref = refs[n1 + n2 + 2 : n1 + n2 + 7]
    first_full, active, grad = refs[n1 + n2 + 7 :]
    tokens, width = inputs.shape
    col, row = lax.axis_index("col"), lax.axis_index("row")
    place, way = place_of(col, columns), 1 - 2 * (row % 2)
    for ref, back in zip(first_refs, first_plan):
        if back is None:
            first_full[...] = ref[...]
        else:
            rows = ref.shape[0]
            start = member_at(place + way * back, columns) * rows
            first_full[pl.ds(pl.multiple_of(start, rows), rows), :] = ref[...]
    for ref, flips in zip(second_refs, second_plan):
        if flips is None:
            second_ref[...] = ref[...]
        else:
            rows = ref.shape[1]
            for k, flip in enumerate(flips):
                second_ref[pl.ds(pl.multiple_of((row ^ flip) * rows, rows), rows), :] = ref[k]
    cut = width // 2 // 128 * 128
    output = 0.0
    for some in (slice(0, cut), slice(cut, width)):
        pre = jnp.dot(inputs[...], first_full[:, some], preferred_element_type=F32)
        value, slope = gelu_and_slope(pre)
        active[:, some] = value.astype(BF16)
        slope_ref[:, some] = slope
        output += jnp.dot(active[:, some], second_ref[some, :], preferred_element_type=F32)
    error = ((output - wanted[...].astype(F32)) / tokens).astype(BF16)
    error_ref[...] = error
    grad[...] = lax.dot_general(
        active[...], error, (((0,), (0,)), ((), ())), preferred_element_type=F32
    ).astype(BF16)
    rows = width // n_row
    if tiled(rows):
        mine = row % 2
        for k in range(n_row // 2):
            for ref, side in ((away, 1 - mine), (kept, mine)):
                ref[k] = grad[pl.ds(pl.multiple_of((2 * k + side) * rows, rows), rows), :]
    else:
        away[...] = grad[: width // 2].reshape(away.shape)
        kept[...] = grad[width // 2 :].reshape(kept.shape)


def backward_kernel(columns, inputs, second_full, error, slope, *refs):
    outs, grad = refs[:-1], refs[-1]
    back = lax.dot_general(
        error[...], second_full[...], (((1,), (1,)), ((), ())), preferred_element_type=F32
    )
    grad_pre = (back * slope[...]).astype(BF16)
    value = lax.dot_general(
        inputs[...], grad_pre, (((0,), (0,)), ((), ())), preferred_element_type=F32
    )
    if len(outs) == 1:
        outs[0][...] = value.astype(BF16)
        return
    grad[...] = value.astype(BF16)
    place, way = place_of(lax.axis_index("col"), columns), 1 - 2 * (lax.axis_index("row") % 2)
    rows = grad.shape[0] // columns

    def block(away):
        start = member_at(place + way * away, columns) * rows
        return grad[pl.ds(pl.multiple_of(start, rows), rows), :]

    *own, other = outs
    for k, ref in enumerate(own):
        ref[...] = block(columns // 2 - k)
    for k in range(other.shape[0]):
        other[k] = block(-(columns // 2 - 1 - k))


def add_kernel(term, came, out):
    out[...] = (term[...].reshape(out.shape).astype(F32) + came[...].astype(F32)).astype(BF16)


def added(term, came):
    if tiled(came.shape[0]):
        return call(add_kernel, [shape_of(came.shape)], [], term, came)[0]
    return (term.reshape(came.shape).astype(F32) + came.astype(F32)).astype(BF16)


def second_kernel(n_row, ahead, kept, came, params, moment, late):
    grad = (kept[0].astype(F32) + came[0].astype(F32)) / n_row
    rows = grad.shape[0]
    late[:ahead] = grad[:ahead].astype(BF16)
    moment_new = outer_momentum * moment[ahead:] + grad[ahead:]
    params_new = params[ahead:] - outer_rate * (grad[ahead:] + outer_momentum * moment_new)
    late[ahead:rows] = params_new.astype(BF16)
    late[rows:] = moment_new.astype(BF16)


def arrive_kernel(early, late, params_out, moment_out):
    ahead, rows = early.shape[1], params_out.shape[0]
    grad = late[:ahead].astype(F32)
    params_out[:ahead] = early[0].astype(F32) - outer_rate * (1 + outer_momentum) * grad
    moment_out[:ahead] = outer_momentum * early[1].astype(F32) + grad
    params_out[ahead:] = late[ahead:rows].astype(F32)
    moment_out[ahead:] = late[rows:].astype(F32)


def closing_kernel(columns, own, ours, theirs, params, moment, params_out, moment_out):
    grad = (own[...].astype(F32) + ours[...].astype(F32) + theirs[...].astype(F32)) / columns
    moment_new = outer_momentum * moment[...] + grad
    moment_out[...] = moment_new
    params_out[...] = params[...] - outer_rate * (grad + outer_momentum * moment_new)


def halve_kernel(bit, kept, came, away_out, kept_out):
    mine = (lax.axis_index("row") // bit) % 2
    for k in range(kept_out.shape[0]):
        total = kept[2 * k + mine].astype(F32) + came[2 * k + mine].astype(F32)
        kept_out[k] = total
        other = kept[2 * k + 1 - mine].astype(F32) + came[2 * k + 1 - mine].astype(F32)
        away_out[k] = other.astype(BF16)


def per_device(hidden_in, targets, first_params, first_moment, second_params, second_moment):
    inputs, wanted = hidden_in[0, 0], targets[0, 0]
    tokens, width = inputs.shape
    columns, n_row = lax.axis_size("col"), lax.axis_size("row")
    offset = columns // 4
    rows1, rows2 = first_params.shape[1], second_params.shape[1]
    ring = two_way(n_row, columns)
    ahead_by = [(i, (i + offset) % columns) for i in range(columns)]
    last = columns // 2
    place = place_of(lax.axis_index("col"), columns)
    row = lax.axis_index("row")
    way = 1 - 2 * (row % 2)
    partner = swap_pairs(n_row, 1)

    ahead = AHEAD * rows2 // 14 // 16 * 16
    own1 = first_params[0].astype(BF16)
    held = second_params[0].astype(BF16)
    early = call(
        prepare_kernel, [shape_of((2, ahead, width))], [], second_params[0], second_moment[0]
    )[0]
    held = held[None]
    first_pieces = [(own1, 0)]
    ours, theirs = own1, lax.ppermute(own1, "row", partner)
    for step in range(1, last + 1):
        later = ours
        ours = lax.ppermute(ours, ("row", "col"), ring)
        first_pieces.append((ours, -step))
        if step < last:
            theirs = lax.ppermute(theirs, ("row", "col"), ring)
            across = lax.ppermute(theirs, "row", partner)
            first_pieces.append((across, step))
    second_pieces, flips = [(held, [0])], [0]
    bit = n_row // 2
    while bit >= 1:
        other = lax.ppermute(held, "row", swap_pairs(n_row, bit))
        others = [f ^ bit for f in flips]
        second_pieces.append((other, others))
        flips = flips + others
        bit = bit // 2
        if bit >= 1:
            other, _ = lax.optimization_barrier((other, later))
            held = jnp.concatenate([held, other])
    early, _ = lax.optimization_barrier((early, theirs))
    early = lax.ppermute(early, "col", ahead_by)
    if tiled(rows1):
        first_blocks, first_plan = [p[0] for p in first_pieces], [p[1] for p in first_pieces]
    else:
        placed = [(b, member_at(place + way * back, columns)) for b, back in first_pieces]
        first_blocks, first_plan = [rows_from(placed, rows1, columns)], [None]
    if tiled(rows2):
        second_plan = [p[1] for p in second_pieces]
        second_blocks = [p[0] for p in second_pieces]
    else:
        placed = [(b[k], row ^ f) for b, fs in second_pieces for k, f in enumerate(fs)]
        second_blocks, second_plan = [rows_from(placed, rows2, n_row)], [None]

    def fwd(*refs):
        forward_kernel(first_plan, second_plan, columns, n_row, *refs)

    part = shape_of((n_row // 2, rows2, width))
    away, kept, error, slope, second_full = call(
        fwd,
        [part, part, shape_of((tokens, width)), shape_of((tokens, width), F32), shape_of((width, width))],
        [pltpu.VMEM((width, width), BF16), pltpu.VMEM((tokens, width), BF16), pltpu.VMEM((width, width), BF16)],
        *first_blocks,
        *second_blocks,
        inputs,
        wanted,
        flops=6 * tokens * width * width,
    )
    if not tiled(rows2):
        pairs = jnp.concatenate([away, kept]).reshape(n_row // 2, 2, rows2, width)
        away = lax.dynamic_index_in_dim(pairs, 1 - row % 2, 1, keepdims=False)
        kept = lax.dynamic_index_in_dim(pairs, row % 2, 1, keepdims=False)
    came = lax.ppermute(away, "row", swap_pairs(n_row, 1))

    def bwd(*refs):
        backward_kernel(columns, *refs)

    block = shape_of((rows1, width))
    outs = [block] * (last + 1) + [shape_of((last - 1, rows1, width))]
    outs = outs if tiled(rows1) else [shape_of((width, width))]
    blocks = call(
        bwd,
        outs,
        [pltpu.VMEM((width, width), BF16)],
        inputs,
        second_full,
        error,
        slope,
        flops=4 * tokens * width * width,
    )
    if not tiled(rows1):
        blocks_full = blocks[0]

        def cut(away):
            start = member_at(place + way * away, columns) * rows1
            return lax.dynamic_slice_in_dim(blocks_full, start, rows1, 0)

        blocks = [cut(last - k) for k in range(last + 1)]
        blocks.append(jnp.stack([cut(-(last - 1 - k)) for k in range(last - 1)]))
    *own_terms, other_terms = blocks

    bit = 2
    while bit < n_row:
        if tiled(rows2):
            n = kept.shape[0] // 2
            away, kept = call(
                lambda *refs, bit=bit: halve_kernel(bit, *refs),
                [shape_of((n, rows2, width)), shape_of((n, rows2, width), F32)],
                [],
                kept,
                came,
            )
        else:
            total = (kept.astype(F32) + came.astype(F32)).reshape(-1, 2, rows2, width)
            mine = (row // bit) % 2
            away = lax.dynamic_index_in_dim(total, 1 - mine, 1, keepdims=False).astype(BF16)
            kept = lax.dynamic_index_in_dim(total, mine, 1, keepdims=False)
        came = lax.ppermute(away, "row", swap_pairs(n_row, bit))
        bit = bit * 2
    late = call(
        lambda *refs: second_kernel(n_row, ahead, *refs),
        [shape_of((2 * rows2 - ahead, width))],
        [],
        kept,
        came,
        second_params[0],
        second_moment[0],
    )[0]
    late = lax.ppermute(late, "col", ahead_by)
    ours = lax.ppermute(own_terms[0], ("row", "col"), ring)
    other_terms = lax.ppermute(other_terms, "row", partner)
    theirs = lax.ppermute(other_terms[0], ("row", "col"), ring)
    for step in range(2, last + 1):
        ours = added(own_terms[step - 1], ours)
        ours = lax.ppermute(ours, ("row", "col"), ring)
        if step < last:
            theirs = added(other_terms[step - 1], theirs)
            theirs = lax.ppermute(theirs, ("row", "col"), ring)
    theirs = lax.ppermute(theirs, "row", partner)

    second_new = call(arrive_kernel, [shape_of((rows2, width), F32)] * 2, [], early, late)
    first_new = call(
        lambda *refs: closing_kernel(columns, *refs),
        [shape_of((rows1, width), F32)] * 2,
        [],
        own_terms[last],
        ours,
        theirs,
        first_params[0],
        first_moment[0],
    )
    return tuple(new[None] for new in (*first_new, *second_new))


def solution(mesh):
    return jax.shard_map(
        per_device,        mesh=mesh,
        in_specs=(
            P("row", "col", None, None),
            P("row", "col", None, None),
            P("row", "col", None),
            P("row", "col", None),
            P("col", "row", None),
            P("col", "row", None),
        ),
        out_specs=(
            P("row", "col", None),
            P("row", "col", None),
            P("col", "row", None),
            P("col", "row", None),
        ),
        check_vma=False,
    )
```
